256 devices in a mesh: rows: 64 (over y, z, core), cols: 4 (over x).
Axes of the slice: x: 4, y: 4, z: 8, core: 2. Of those that a mesh axis runs over, the one named last changes fastest.
Arguments:
- residual_block: float32 [524288, 64], P('rows', 'cols'), may hold values from -6 to 6
- basis: bfloat16 [524288, 64], P('rows', 'cols'), may hold values from -0.0078125 to 0.0078125
- fine_tiles: bfloat16 [4096, 4, 128, 128], P('rows')
- fine_index: int32 [4096, 4], P('rows'), may hold values from 0 to 4095, as said below
- mid_tiles: bfloat16 [512, 3, 128, 128], P('rows')
- fine_owner: int32 [524288], P('rows'), may hold values from 0 to 65535, as said below
- mid_owner: int32 [65536], P('rows'), may hold values from 0 to 8191, as said below
- coarse_inverse: float32 [8192, 8192], P('rows'), as said below
Outputs:
- directions: float32 [524288, 64], P('rows', 'cols')
- gram: float32 [64, 64], P(None, 'cols')
The draws below stay inside these ranges and needn't reach their ends.
Inputs may be any that keep to these rules, and one draw needn't show every extreme that they name: `fine_index`: slot 0 of block row g names g itself; every block named in a block row of partition p (block rows p*64 to p*64 + 63) belongs to partition p - 1, p or p + 1. `fine_owner`: the fine vertices of partition p map to level-one rows p*1024 to p*1024 + 1023; every level-one row receives exactly 8 vertices. `mid_owner`: the level-one rows of partitions 2q and 2q + 1 map to level-two rows 2q*128 to 2q*128 + 2*128 - 1; every level-two row receives exactly 8 level-one rows. coarse_inverse is symmetric.
All inputs are finite; a program needn't handle non-finite values.
Results may differ from the reference program's by a relative error of at most 0.013.
Values may be sent and summed in bfloat16 or wider, within the bound.
A program may use at most 64 MiB of HBM per device.

```python
import math
import jax
import jax.numpy as jnp
from jax import lax

BLOCK = 128
SLOTS = 4
COLUMNS = 64
BLOCKS_DEV = 64
FINE_BLOCKS = 4096
FINE_ROWS = 524288
MID_DEV = 1024
MID_BLOCKS = 512
MID_ROWS = 65536
COARSE_DEV = 128
COARSE_ROWS = 8192
N_ROWS = 64


def tile_draw(key, blocks, slots, diag_slot):
    shape = (blocks, slots, BLOCK, BLOCK)
    spread = 1.1 / math.sqrt(slots * BLOCK)
    noise = jax.random.truncated_normal(key, -4.0, 4.0, shape, jnp.float32) * spread
    level = jax.random.uniform(jax.random.fold_in(key, 1), (blocks, 1, BLOCK, 1), jnp.float32, 1.5, 3.0)
    diag_rows = lax.broadcasted_iota(jnp.int32, (1, slots, BLOCK, BLOCK), 2)
    diag_cols = lax.broadcasted_iota(jnp.int32, (1, slots, BLOCK, BLOCK), 3)
    slot_ids = lax.broadcasted_iota(jnp.int32, (1, slots, BLOCK, BLOCK), 1)
    marked = ((diag_rows == diag_cols) & (slot_ids == diag_slot)).astype(jnp.float32)
    return (noise + level * marked).astype(jnp.bfloat16)


def draw_fine_tiles(key, part):
    return tile_draw(key, FINE_BLOCKS, SLOTS, 0)


def draw_mid_tiles(key, part):
    return tile_draw(key, MID_BLOCKS, 3, 1)


def draw_fine_index(key, part):
    rows_id = lax.iota(jnp.int32, FINE_BLOCKS)
    part_id = rows_id // BLOCKS_DEV
    base = part_id * BLOCKS_DEV
    left_pick = jax.random.randint(jax.random.fold_in(key, 11), (FINE_BLOCKS,), 0, BLOCKS_DEV)
    right_pick = jax.random.randint(jax.random.fold_in(key, 12), (FINE_BLOCKS,), 0, BLOCKS_DEV)
    inner_pick = jax.random.randint(jax.random.fold_in(key, 13), (FINE_BLOCKS,), 0, BLOCKS_DEV)
    left = jnp.where(part_id > 0, base - BLOCKS_DEV + left_pick, base + left_pick)
    right = jnp.where(part_id < N_ROWS - 1, base + BLOCKS_DEV + right_pick, base + right_pick)
    inner = base + inner_pick
    return jnp.stack([rows_id, left, right, inner], axis=1).astype(jnp.int32)


def draw_fine_owner(key, part):
    keys = jax.random.split(key, N_ROWS)

    def shuffled(single):
        return jax.random.permutation(single, BLOCKS_DEV * BLOCK) // 8
    local = jax.vmap(shuffled)(keys).astype(jnp.int32)
    offsets = lax.iota(jnp.int32, N_ROWS)[:, None] * MID_DEV
    return (local + offsets).reshape(-1).astype(jnp.int32)


def draw_mid_owner(key, part):
    pairs = N_ROWS // 2
    keys = jax.random.split(key, pairs)

    def shuffled(single):
        return jax.random.permutation(single, 2 * MID_DEV) // 8
    local = jax.vmap(shuffled)(keys).astype(jnp.int32)
    offsets = lax.iota(jnp.int32, pairs)[:, None] * (2 * COARSE_DEV)
    return (local + offsets).reshape(-1).astype(jnp.int32)


def draw_coarse_inverse(key, part):
    shape = (COARSE_ROWS, COARSE_ROWS)
    raw = jax.random.normal(key, shape, jnp.float32)
    mixed = (raw + raw.T) * (0.5 / math.sqrt(COARSE_ROWS))
    leading = jax.random.uniform(jax.random.fold_in(key, 3), (COARSE_ROWS,), jnp.float32, 0.2, 0.6)
    return mixed + jnp.diag(leading)


def shard_levels(rng, dims, pieces, low, largest):
    factor_of, own = 1.0, jax.random.fold_in(rng, 6)
    for axis_at, blocks in pieces:
        steps = jnp.exp(jax.random.uniform(jax.random.fold_in(own, axis_at), (blocks,), jnp.float32, low / len(pieces), largest / len(pieces)))
        factor_of = factor_of * jnp.repeat(steps, dims[axis_at] // blocks).reshape([-1 if axis == axis_at else 1 for axis in range(len(dims))])
    return factor_of


def scatter_about(key, dims, scale, reach, cuts=(), held_as=jnp.bfloat16):
    result = jax.random.normal(key, dims, jnp.float32) * scale
    if len(cuts) > 0:
        result = shard_levels(key, dims, cuts, -0.22, 0.18) * result
    return jnp.clip(result, min=-reach, max=reach).astype(held_as)


def setup_inputs(seed: int = 0) -> dict:
    arg_keys = jax.random.split(jax.random.key(seed), 9)
    residual_block = scatter_about(arg_keys[0], (FINE_ROWS, COLUMNS), 1.0, 6.0, ((0, 64), (1, 4)), jnp.float32)
    basis = scatter_about(arg_keys[1], (FINE_ROWS, COLUMNS), FINE_ROWS ** -0.5, 0.0078125, ((0, 64), (1, 4)))
    fine_tiles = draw_fine_tiles(jax.random.fold_in(arg_keys[8], 71), 0)
    fine_index = draw_fine_index(jax.random.fold_in(arg_keys[8], 71), 0)
    mid_tiles = draw_mid_tiles(jax.random.fold_in(arg_keys[8], 71), 0)
    fine_owner = draw_fine_owner(jax.random.fold_in(arg_keys[8], 71), 0)
    mid_owner = draw_mid_owner(jax.random.fold_in(arg_keys[8], 71), 0)
    coarse_inverse = draw_coarse_inverse(jax.random.fold_in(arg_keys[8], 71), 0)
    return dict(residual_block=residual_block, basis=basis, fine_tiles=fine_tiles, fine_index=fine_index, mid_tiles=mid_tiles, fine_owner=fine_owner, mid_owner=mid_owner, coarse_inverse=coarse_inverse)


DAMPING = 0.6666666666666666


def fine_apply(matrix, slot_index, vector):
    packed = lax.optimization_barrier(vector.astype(jnp.bfloat16)).reshape(FINE_BLOCKS, BLOCK, COLUMNS)
    tile_groups = matrix.reshape(N_ROWS, BLOCKS_DEV, SLOTS, BLOCK, BLOCK)
    index_groups = slot_index.reshape(N_ROWS, BLOCKS_DEV, SLOTS)

    def one_group(bundle):
        group_tiles, group_index = bundle
        picked = packed[group_index].astype(jnp.float32)
        return jnp.einsum("bkij,bkjc->bic", group_tiles.astype(jnp.float32), picked)

    product = lax.map(one_group, (tile_groups, index_groups))
    return product.reshape(FINE_ROWS, COLUMNS)


def mid_apply(matrix, vector):
    packed = lax.optimization_barrier(vector.astype(jnp.bfloat16)).astype(jnp.float32)
    packed = packed.reshape(MID_BLOCKS, BLOCK, COLUMNS)
    padded = jnp.pad(packed, ((1, 1), (0, 0), (0, 0)))
    wide = matrix.astype(jnp.float32)
    product = jnp.einsum("bij,bjc->bic", wide[:, 0], padded[:-2])
    product = product + jnp.einsum("bij,bjc->bic", wide[:, 1], padded[1:-1])
    product = product + jnp.einsum("bij,bjc->bic", wide[:, 2], padded[2:])
    return product.reshape(MID_ROWS, COLUMNS)


def reference(residual_block, basis, fine_tiles, fine_index, mid_tiles, fine_owner, mid_owner, coarse_inverse):
    fine_inv = 1.0 / jnp.diagonal(fine_tiles[:, 0], axis1=1, axis2=2).astype(jnp.float32).reshape(FINE_ROWS, 1)
    mid_inv = 1.0 / jnp.diagonal(mid_tiles[:, 1], axis1=1, axis2=2).astype(jnp.float32).reshape(MID_ROWS, 1)
    fine_x = DAMPING * fine_inv * residual_block
    fine_x = fine_x + DAMPING * fine_inv * (residual_block - fine_apply(fine_tiles, fine_index, fine_x))
    fine_res = residual_block - fine_apply(fine_tiles, fine_index, fine_x)
    mid_rhs = jax.ops.segment_sum(fine_res, fine_owner, num_segments=MID_ROWS)
    mid_x = DAMPING * mid_inv * mid_rhs
    mid_x = mid_x + DAMPING * mid_inv * (mid_rhs - mid_apply(mid_tiles, mid_x))
    mid_res = mid_rhs - mid_apply(mid_tiles, mid_x)
    coarse_rhs = jax.ops.segment_sum(mid_res, mid_owner, num_segments=COARSE_ROWS)
    coarse_fix = jnp.dot(coarse_inverse, coarse_rhs, precision=lax.Precision.HIGHEST)
    mid_x = mid_x + coarse_fix[mid_owner]
    mid_x = mid_x + DAMPING * mid_inv * (mid_rhs - mid_apply(mid_tiles, mid_x))
    fine_x = fine_x + mid_x[fine_owner]
    directions = fine_x + DAMPING * fine_inv * (residual_block - fine_apply(fine_tiles, fine_index, fine_x))
    gram = jnp.dot(basis.T, directions.astype(jnp.bfloat16), preferred_element_type=jnp.float32)
    return directions, gram
```

```python
import functools

import jax
import jax.numpy as jnp
from jax import lax
from jax.experimental import pallas as pl
from jax.experimental.pallas import tpu as pltpu
from jax.sharding import PartitionSpec as P

W = 0.6666666666666666
NT = (((1,), (1,)), ((), ()))
NN = (((1,), (0,)), ((), ()))
F32 = jnp.float32
BF = jnp.bfloat16
L = 128
QUARTERS = 4


def dot(a, b, dims):
    return lax.dot_general(a, b, dims, preferred_element_type=F32)


def split(x):
    high = x.astype(BF)
    return high, (x - high.astype(F32)).astype(BF)


def kernel(
    ny, nz, nx,
    res_hbm, basis_hbm, tiles_hbm, idx_ref, mid_hbm, own_hbm, mown_hbm, coarse_hbm,
    dir_ref, gram_ref,
    res_v, tiles_v, mid_v, own_v, mown_v, coarse_v, cb_v, basis_v, scale_v, x_v, fr_v,
    win1, win2, win3, oht, oh2t, ms_v, mwin1, mwin2, mwin3, pair1, pair2, ag, cw, dirb,
    ga, gz, gy,
    lsem, hs, hr, msend, mrecv, psend, precv, ags, agr, bs, br, gs, gr,
):
    nb = tiles_v.shape[0]
    nm = mid_v.shape[0]
    nch = ny * nz
    rows = 2 * nch
    cdev = coarse_v.shape[0]
    cols = res_v.shape[0]
    r = lax.axis_index("rows")
    x = lax.axis_index("cols")
    core = lax.rem(r, 2)
    chip = r // 2
    zc = lax.rem(chip, nz)
    yc = chip // nz
    right = lax.rem(r + 1, rows)
    left = lax.rem(r + rows - 1, rows)
    partner = 2 * chip + 1 - core
    outer = lax.rem(r + 2 * core - 1 + rows, rows)

    def remote(src, dst, ssem, rsem, where):
        return pltpu.make_async_remote_copy(
            src_ref=src, dst_ref=dst, send_sem=ssem, recv_sem=rsem,
            device_id=where, device_id_type=pl.DeviceIdType.MESH,
        )

    def local(src, dst, k):
        return pltpu.make_async_copy(src, dst, lsem.at[k])

    def lanes(g, n=1):
        return pl.ds(pl.multiple_of(g * L, L), n * L)

    diag_in = local(tiles_hbm.at[:, 0], tiles_v.at[:, 0], 0)
    res_in = local(res_hbm, res_v, 1)
    off_in = local(tiles_hbm.at[:, 1:4], tiles_v.at[:, 1:4], 2)
    own_in = local(own_hbm, own_v, 3)
    mown_in = local(mown_hbm, mown_v, 4)
    mid_in = local(mid_hbm, mid_v, 5)
    coarse_in = local(coarse_hbm, coarse_v, 6)
    basis_in = local(basis_hbm, basis_v.at[x], 7)
    for copy in (diag_in, res_in, own_in, mown_in, off_in, mid_in, coarse_in, basis_in):
        copy.start()

    barrier = pltpu.get_barrier_semaphore()

    def greet(where):
        pl.semaphore_signal(
            barrier, inc=1, device_id=where, device_id_type=pl.DeviceIdType.MESH
        )

    greet({"rows": partner})
    greet({"rows": outer})

    @pl.loop(1, nch)
    def _(d):
        greet({"rows": 2 * lax.rem(chip + d, nch) + core})

    @pl.loop(1, nx)
    def _(d):
        greet({"cols": lax.rem(x + d, nx)})

    eye = lax.broadcasted_iota(jnp.int32, (L, L), 0) == lax.broadcasted_iota(
        jnp.int32, (L, L), 1
    )

    def weight(tile):
        d = jnp.sum(jnp.where(eye, tile.astype(F32), 0.0), axis=0, keepdims=True)
        return jnp.broadcast_to(W * (1.0 / d), (cols, L))

    diag_in.wait()
    res_in.wait()

    def first(g, carry):
        s = weight(tiles_v[g, 0])
        scale_v[g] = s
        win1[nb + g] = (s * res_v[:, lanes(g)]).astype(BF)
        return carry

    lax.fori_loop(0, nb, first, 0, unroll=4)

    def halo(win, k, lo, n):
        return (
            remote(win.at[pl.ds(nb + lo, n)], win.at[pl.ds(lo, n)], hs.at[k, 0], hr.at[k, 0], {"rows": right}),
            remote(win.at[pl.ds(nb + lo, n)], win.at[pl.ds(2 * nb + lo, n)], hs.at[k, 1], hr.at[k, 1], {"rows": left}),
        )

    def halo_start(win, k, lo, n):
        for copy in halo(win, k, lo, n):
            copy.start()

    def halo_wait(win, k):
        for copy in halo(win, k, 0, nb):
            copy.wait_recv()

    pl.semaphore_wait(barrier, nch - 1 + 2 + nx - 1)
    halo_start(win1, 0, 0, nb)

    basis_in.wait()

    def basis_copy(d):
        return remote(
            basis_v.at[x], basis_v.at[x], bs, br, {"cols": lax.rem(x + d, nx)}
        )

    @pl.loop(1, nx)
    def _(d):
        basis_copy(d).start()

    own_in.wait()
    mown_in.wait()
    mid_in.wait()
    low_iota = lax.broadcasted_iota(jnp.int32, (L, L), 0)
    fine_base = r * (nm * L)

    def owner_row(g):
        return own_v[pl.ds(g, 1), :] - fine_base

    def hot(g, carry):
        low = jnp.bitwise_and(owner_row(g), L - 1)
        oht[:, lanes(g)] = jnp.where(low_iota == low, 1.0, 0.0).astype(BF)
        return carry

    lax.fori_loop(0, nb, hot, 0, unroll=4)
    wide_iota = lax.broadcasted_iota(jnp.int32, (2 * cdev, L), 0)
    mid_base = (r - core) * cdev
    for g in range(nm):
        oh2t[:, g * L : (g + 1) * L] = jnp.where(
            wide_iota == mown_v[g : g + 1, :] - mid_base, 1.0, 0.0
        ).astype(BF)
        ms_v[g] = weight(mid_v[g, 1])

    off_in.wait()
    halo_wait(win1, 0)
    base = (r - 1) * nb

    def product(win, g):
        picked = [win[nb + g]] + [
            win[jnp.clip(idx_ref[s, g] - base, 0, 3 * nb - 1)] for s in (1, 2, 3)
        ]
        tile = [tiles_v[g, s] for s in range(4)]
        return dot(jnp.concatenate(picked, axis=1), jnp.concatenate(tile, axis=1), NT)

    def fine_b(g, carry):
        s = scale_v[g]
        rhs = res_v[:, lanes(g)]
        v = s * rhs + s * (rhs - product(win1, g))
        x_v[g] = v
        win2[nb + g] = v.astype(BF)
        return carry

    step = nb // QUARTERS
    for q in range(QUARTERS):
        lax.fori_loop(q * step, (q + 1) * step, fine_b, 0, unroll=min(8, step))
        halo_start(win2, 1, q * step, step)

    coarse_in.wait()

    def convert(c, carry):
        for k in range(2):
            at = pl.multiple_of((2 * c + k) * cdev, cdev)
            cb_v[k, c] = coarse_v[:, pl.ds(at, cdev)].astype(BF)
        return carry

    lax.fori_loop(0, nch, convert, 0, unroll=2)
    halo_wait(win2, 1)

    def residual(g, carry):
        fr_v[g] = res_v[:, lanes(g)] - product(win2, g)
        return carry

    lax.fori_loop(0, nb, residual, 0, unroll=8)

    def restrict(c, acc):
        parts = []
        for k in range(4):
            g = 4 * c + k
            high = jnp.broadcast_to(lax.shift_right_logical(owner_row(g), 7), (cols, L))
            v = fr_v[g]
            parts.append(
                jnp.concatenate(
                    [jnp.where(high == h, v, 0.0).astype(BF) for h in range(nm)], axis=0
                )
            )
        return acc + dot(jnp.concatenate(parts, axis=1), oht[:, lanes(4 * c, 4)], NT)

    mid_rhs = lax.fori_loop(
        0, nb // 4, restrict, jnp.zeros((nm * cols, L), F32), unroll=2
    ).reshape(nm, cols, L)

    ms = ms_v[...]

    def mid_halo(mwin, k):
        return (
            remote(mwin.at[nm], mwin.at[0], msend.at[k, 0], mrecv.at[k, 0], {"rows": right}),
            remote(mwin.at[1], mwin.at[nm + 1], msend.at[k, 1], mrecv.at[k, 1], {"rows": left}),
        )

    def mid_product(v, mwin, k):
        mwin[1 : nm + 1] = v.astype(BF)
        for copy in mid_halo(mwin, k):
            copy.start()
        for copy in mid_halo(mwin, k):
            copy.wait_recv()
        zero = jnp.zeros((cols, L), BF)
        mwin[0] = jnp.where(r > 0, mwin[0], zero)
        mwin[nm + 1] = jnp.where(r < rows - 1, mwin[nm + 1], zero)
        out = []
        for g in range(nm):
            v3 = jnp.concatenate([mwin[g + k] for k in range(3)], axis=1)
            t3 = jnp.concatenate([mid_v[g, k] for k in range(3)], axis=1)
            out.append(dot(v3, t3, NT))
        return jnp.stack(out)

    mid_x = ms * mid_rhs
    mid_x = mid_x + ms * (mid_rhs - mid_product(mid_x, mwin1, 0))
    mid_res = mid_rhs - mid_product(mid_x, mwin2, 1)

    def flat(v):
        return jnp.concatenate([v[g] for g in range(nm)], axis=1)

    both = dot(jnp.concatenate(split(flat(mid_res)), axis=0), oh2t[...], NT)
    partial = both[:cols] + both[cols:]
    even, odd = partial[:, :cdev], partial[:, cdev:]
    pair1[0] = jnp.where(core == 0, odd, even)
    swap1 = remote(pair1.at[0], pair1.at[1], psend.at[0], precv.at[0], {"rows": partner})
    swap1.start()
    swap1.wait_recv()
    coarse_rhs = jnp.where(core == 0, even, odd) + pair1[1]

    ag[core, chip] = coarse_rhs.astype(BF)

    def ag_copy(d):
        return remote(
            ag.at[core, chip], ag.at[core, chip], ags.at[0], agr.at[0],
            {"rows": 2 * lax.rem(chip + d, nch) + core},
        )

    @pl.loop(1, nch)
    def _(d):
        ag_copy(d).start()

    def ag_rest(slot):
        return remote(
            ag.at[slot, pl.ds(0, nch - 1)], ag.at[slot, pl.ds(0, nch - 1)],
            ags.at[0], agr.at[0], {"rows": partner},
        )

    ag_rest(core).wait_recv()
    half = remote(ag.at[core], ag.at[core], ags.at[1], agr.at[1], {"rows": partner})
    half.start()

    def coarse_half(k, acc):
        def chunk(c, acc):
            v = jnp.concatenate([ag[k, 4 * c + i] for i in range(4)], axis=1)
            t = jnp.concatenate([cb_v[k, 4 * c + i] for i in range(4)], axis=1)
            return acc + dot(v, t, NT)

        return lax.fori_loop(0, nch // 4, chunk, acc, unroll=min(4, nch // 4))

    fix = coarse_half(core, jnp.zeros((cols, cdev), F32))
    half.wait_recv()
    fix = coarse_half(1 - core, fix)

    pair2[0] = fix
    swap2 = remote(pair2.at[0], pair2.at[1], psend.at[1], precv.at[1], {"rows": partner})
    swap2.start()
    swap2.wait_recv()
    other = pair2[1]
    values = jnp.concatenate(
        [jnp.where(core == 0, fix, other), jnp.where(core == 0, other, fix)], axis=1
    )
    both = dot(jnp.concatenate(split(values), axis=0), oh2t[...], NN)
    lift = both[:cols] + both[cols:]
    mid_x = mid_x + jnp.stack([lift[:, g * L : (g + 1) * L] for g in range(nm)])
    mid_x = mid_x + ms * (mid_rhs - mid_product(mid_x, mwin3, 2))

    md = mid_x.reshape(nm * cols, L)
    cw[...] = jnp.concatenate(split(md), axis=1)

    def prolong(c, carry):
        hot4 = oht[:, lanes(4 * c, 4)]
        up = dot(cw[...], jnp.concatenate([hot4, hot4], axis=0), NN)
        for k in range(4):
            g = 4 * c + k
            high = jnp.broadcast_to(lax.shift_right_logical(owner_row(g), 7), (cols, L))
            v = x_v[g]
            for h in range(nm):
                v = v + jnp.where(
                    high == h, up[h * cols : (h + 1) * cols, k * L : (k + 1) * L], 0.0
                )
            x_v[g] = v
            win3[nb + g] = v.astype(BF)
        return carry

    for q in range(QUARTERS):
        lax.fori_loop(q * step // 4, (q + 1) * step // 4, prolong, 0, unroll=min(2, step // 4))
        halo_start(win3, 2, q * step, step)
    halo_wait(win3, 2)

    def finish(g, carry):
        v = x_v[g] + scale_v[g] * (res_v[:, lanes(g)] - product(win3, g))
        dir_ref[:, lanes(g)] = v
        dirb[:, lanes(g)] = v.astype(BF)
        return carry

    lax.fori_loop(0, nb, finish, 0, unroll=8)

    def basis_rest():
        return remote(
            basis_v.at[pl.ds(0, nx - 1)], basis_v.at[pl.ds(0, nx - 1)], bs, br,
            {"rows": partner},
        )

    basis_rest().wait_recv()

    def gram(c, acc):
        t = basis_v[:, :, lanes(4 * c, 4)].reshape(nx * cols, 4 * L)
        return acc + dot(dirb[:, lanes(4 * c, 4)], t, NT)

    total = lax.fori_loop(
        0, nb // 4, gram, jnp.zeros((cols, nx * cols), F32), unroll=min(4, nb // 4)
    )
    rows8 = cols // 2
    ga[core] = jnp.concatenate([total[:rows8], total[rows8:]], axis=1)
    swap3 = remote(ga.at[core], ga.at[core], gs.at[0], gr.at[0], {"rows": partner})
    swap3.start()
    swap3.wait_recv()
    gz[zc] = ga[0] + ga[1]

    def z_copy(d):
        to = 2 * (yc * nz + lax.rem(zc + d, nz)) + core
        return remote(gz.at[zc], gz.at[zc], gs.at[1], gr.at[1], {"rows": to})

    def y_copy(d):
        to = 2 * (lax.rem(yc + d, ny) * nz + zc) + core
        return remote(gy.at[yc], gy.at[yc], gs.at[2], gr.at[2], {"rows": to})

    def rest(buf, k, n):
        return remote(
            buf.at[pl.ds(0, n - 1)], buf.at[pl.ds(0, n - 1)], gs.at[k], gr.at[k],
            {"rows": partner},
        )

    @pl.loop(1, nz)
    def _(d):
        z_copy(d).start()

    rest(gz, 1, nz).wait_recv()
    acc = gz[0]
    for k in range(1, nz):
        acc = acc + gz[k]
    gy[yc] = acc

    @pl.loop(1, ny)
    def _(d):
        y_copy(d).start()

    rest(gy, 2, ny).wait_recv()
    acc = gy[0]
    for k in range(1, ny):
        acc = acc + gy[k]
    wide = nx * cols
    gram_ref[...] = jnp.concatenate([acc[:, :wide], acc[:, wide:]], axis=0)

    for k, win in enumerate((win1, win2, win3)):
        for copy in halo(win, k, 0, nb):
            copy.wait_send()
    for k, mwin in enumerate((mwin1, mwin2, mwin3)):
        for copy in mid_halo(mwin, k):
            copy.wait_send()
    for copy in (swap1, swap2, swap3, half, ag_rest(core), basis_rest(), rest(gz, 1, nz), rest(gy, 2, ny)):
        copy.wait_send()


def on_device(ny, nz, nx, residual, basis, fine_tiles, fine_index, mid_tiles, fine_owner, mid_owner, coarse):
    nb = fine_tiles.shape[0]
    nm = mid_tiles.shape[0]
    cols = residual.shape[1]
    cdev = coarse.shape[0]
    n = nb * L
    nch = ny * nz
    vm, dma = pltpu.VMEM, pltpu.SemaphoreType.DMA
    scratch = [
        vm((cols, n), F32), vm((nb, 4, L, L), BF), vm((nm, 3, L, L), BF),
        vm((nb, L), jnp.int32), vm((nm, L), jnp.int32),
        vm(coarse.shape, F32), vm((2, nch, cdev, cdev), BF), vm((nx, cols, n), BF),
        vm((nb, cols, L), F32), vm((nb, cols, L), F32), vm((nb, cols, L), F32),
        vm((3 * nb, cols, L), BF), vm((3 * nb, cols, L), BF), vm((3 * nb, cols, L), BF),
        vm((L, n), BF), vm((2 * cdev, nm * L), BF), vm((nm, cols, L), F32),
        vm((nm + 2, cols, L), BF), vm((nm + 2, cols, L), BF), vm((nm + 2, cols, L), BF),
        vm((2, cols, cdev), F32), vm((2, cols, cdev), F32), vm((2, nch, cols, cdev), BF),
        vm((nm * cols, 2 * L), BF), vm((cols, n), BF),
        vm((2, cols // 2, 2 * nx * cols), F32), vm((nz, cols // 2, 2 * nx * cols), F32),
        vm((ny, cols // 2, 2 * nx * cols), F32),
        dma((8,)), dma((3, 2)), dma((3, 2)), dma((3, 2)), dma((3, 2)), dma((2,)), dma((2,)),
        dma((2,)), dma((2,)), dma, dma, dma((3,)), dma((3,)),
    ]
    hbm = pl.BlockSpec(memory_space=pl.ANY)
    vmem = pl.BlockSpec(memory_space=pltpu.VMEM)
    directions, gram = pl.pallas_call(
        functools.partial(kernel, ny, nz, nx),
        out_shape=(
            jax.ShapeDtypeStruct((cols, n), F32),
            jax.ShapeDtypeStruct((cols, nx * cols), F32),
        ),
        in_specs=[hbm, hbm, hbm, pl.BlockSpec(memory_space=pltpu.SMEM), hbm, hbm, hbm, hbm],
        out_specs=(vmem, vmem),
        scratch_shapes=scratch,
        name="vcycle",
        compiler_params=pltpu.CompilerParams(
            collective_id=0, has_side_effects=True, vmem_limit_bytes=56 * 2**20
        ),
    )(
        residual.T, basis.T, fine_tiles, fine_index.T, mid_tiles,
        fine_owner.reshape(nb, L), mid_owner.reshape(nm, L), coarse,
    )
    return directions.T, gram.T


def solution(mesh, ny=4, nz=8):
    in_specs = (
        P("rows", "cols"),
        P("rows", "cols"),
        P("rows", None, None, None),
        P("rows", None),
        P("rows", None, None, None),
        P("rows"),
        P("rows"),
        P("rows", None),
    )
    out_specs = (P("rows", "cols"), P(None, "cols"))
    return jax.shard_map(
        functools.partial(on_device, ny, nz, mesh.shape["cols"]),
        mesh=mesh, in_specs=in_specs, out_specs=out_specs, check_vma=False,
    )
```

```python
import functools

import jax
import jax.numpy as jnp
from jax import lax
from jax.experimental import pallas as pl
from jax.experimental.pallas import tpu as pltpu
from jax.sharding import PartitionSpec as P

W = 0.6666666666666666
NT = (((1,), (1,)), ((), ()))
NN = (((1,), (0,)), ((), ()))
F32 = jnp.float32
BF = jnp.bfloat16
L = 128
QUARTERS = 4


def dot(a, b, dims):
    return lax.dot_general(a, b, dims, preferred_element_type=F32)


def split(x):
    high = x.astype(BF)
    return high, (x - high.astype(F32)).astype(BF)


def kernel(
    ny, nz, nx,
    res_hbm, basis_hbm, tiles_hbm, idx_ref, mid_hbm, own_hbm, mown_hbm, coarse_hbm,
    dir_ref, gram_ref,
    res_v, tiles_v, mid_v, own_v, mown_v, coarse_v, cb_v, basis_v, scale_v, x_v, fr_v,
    win1, win2, win3, oht, oh2t, ms_v, mrhs, mwin1, mwin2, mwin3, pair1, fx, ag, cw, dirb,
    ga, gd, dir_v, gram_v,
    lsem, dsem, hs, hr, es, er, msend, mrecv, psend, precv, fs, fr, ags, agr, bs, br, gs, gr,
):
    nb = tiles_v.shape[0]
    nm = mid_v.shape[0] - 2
    nch = ny * nz
    rows = 2 * nch
    cdev = coarse_v.shape[0]
    cols = res_v.shape[0]
    r = lax.axis_index("rows")
    x = lax.axis_index("cols")
    core = lax.rem(r, 2)
    chip = r // 2
    right = lax.rem(r + 1, rows)
    left = lax.rem(r + rows - 1, rows)
    partner = 2 * chip + 1 - core
    outer = lax.rem(r + 2 * core - 1 + rows, rows)
    outer2 = 2 * lax.rem(chip + 1 - 2 * core + nch, nch) + core
    step = nb // QUARTERS

    def remote(src, dst, ssem, rsem, where):
        return pltpu.make_async_remote_copy(
            src_ref=src, dst_ref=dst, send_sem=ssem, recv_sem=rsem,
            device_id=where, device_id_type=pl.DeviceIdType.MESH,
        )

    def local(src, dst, k):
        return pltpu.make_async_copy(src, dst, lsem.at[k])

    def lanes(g, n=1):
        return pl.ds(pl.multiple_of(g * L, L), n * L)

    pending = []

    def send(copy):
        copy.start()
        pending.append(copy)

    def pending_done():
        for copy in pending:
            copy.wait_send()

    def diag_in(q):
        at = pl.ds(q * step, step)
        return pltpu.make_async_copy(tiles_hbm.at[at, 0], tiles_v.at[at, 0], dsem.at[q])

    res_in = local(res_hbm, res_v, 1)
    off_in = local(tiles_hbm.at[:, 1:4], tiles_v.at[:, 1:4], 2)
    own_in = local(own_hbm, own_v, 3)
    mown_in = local(mown_hbm, mown_v, 4)
    mid_in = local(mid_hbm, mid_v.at[pl.ds(1, nm)], 5)
    coarse_in = local(coarse_hbm, coarse_v, 6)
    basis_in = local(basis_hbm, basis_v.at[x], 7)
    res_in.start()
    for q in range(QUARTERS):
        diag_in(q).start()
    for copy in (mid_in, own_in, mown_in, off_in, coarse_in, basis_in):
        copy.start()

    barrier = pltpu.get_barrier_semaphore()

    def greet(where):
        pl.semaphore_signal(
            barrier, inc=1, device_id=where, device_id_type=pl.DeviceIdType.MESH
        )

    greet({"rows": partner})
    greet({"rows": outer})

    @pl.loop(1, nch)
    def _(d):
        greet({"rows": 2 * lax.rem(chip + d, nch) + core})

    @pl.loop(1, nx)
    def _(d):
        greet({"cols": lax.rem(x + d, nx)})

    eye = lax.broadcasted_iota(jnp.int32, (L, L), 0) == lax.broadcasted_iota(
        jnp.int32, (L, L), 1
    )

    def weight(tile):
        d = jnp.sum(jnp.where(eye, tile.astype(F32), 0.0), axis=0, keepdims=True)
        return jnp.broadcast_to(W * (1.0 / d), (cols, L))

    def halo(win, k, lo, n):
        return (
            remote(win.at[pl.ds(nb + lo, n)], win.at[pl.ds(lo, n)], hs.at[k, 0], hr.at[k, 0], {"rows": right}),
            remote(win.at[pl.ds(nb + lo, n)], win.at[pl.ds(2 * nb + lo, n)], hs.at[k, 1], hr.at[k, 1], {"rows": left}),
        )

    def halo_start(win, k, lo, n):
        for copy in halo(win, k, lo, n):
            copy.start()
        if lo == 0:
            pending.extend(halo(win, k, 0, nb))

    def halo_wait(win, k):
        for copy in halo(win, k, 0, nb):
            copy.wait_recv()

    def first(g, carry):
        s = weight(tiles_v[g, 0])
        scale_v[g] = s
        win1[nb + g] = (s * res_v[:, lanes(g)]).astype(BF)
        return carry

    res_in.wait()
    for q in range(QUARTERS):
        diag_in(q).wait()
        lax.fori_loop(q * step, (q + 1) * step, first, 0, unroll=min(8, step))
        if q == 0:
            pl.semaphore_wait(barrier, nch - 1 + 2 + nx - 1)
        halo_start(win1, 0, q * step, step)

    basis_in.wait()

    def basis_copy(d):
        return remote(
            basis_v.at[x], basis_v.at[x], bs, br, {"cols": lax.rem(x + d, nx)}
        )

    @pl.loop(1, nx)
    def _(d):
        basis_copy(d).start()

    basis_all = remote(
        basis_v.at[pl.ds(0, nx - 1)], basis_v.at[pl.ds(0, nx - 1)], bs, br,
        {"rows": partner},
    )
    pending.append(basis_all)

    mid_in.wait()
    mown_in.wait()
    wide_iota = lax.broadcasted_iota(jnp.int32, (2 * cdev, L), 0)
    mid_base = (r - core) * cdev
    for g in range(nm):
        oh2t[1 + g] = jnp.where(
            wide_iota == mown_v[g : g + 1, :] - mid_base, 1.0, 0.0
        ).astype(BF)
        ms_v[2 + g] = weight(mid_v[1 + g, 1])
    edges = []
    for k, (buf, n, lo, hi) in enumerate(((mid_v, 1, 1, nm), (oh2t, 1, 1, nm), (ms_v, 2, 2, nm))):
        edges.append(
            remote(buf.at[pl.ds(hi, n)], buf.at[pl.ds(0, n)], es.at[k, 0], er.at[k, 0], {"rows": right})
        )
        edges.append(
            remote(buf.at[pl.ds(lo, n)], buf.at[pl.ds(lo + nm, n)], es.at[k, 1], er.at[k, 1], {"rows": left})
        )
    for copy in edges:
        send(copy)

    own_in.wait()
    low_iota = lax.broadcasted_iota(jnp.int32, (L, L), 0)
    fine_base = r * (nm * L)

    def owner_row(g):
        return own_v[pl.ds(g, 1), :] - fine_base

    def hot(g, carry):
        low = jnp.bitwise_and(owner_row(g), L - 1)
        oht[:, lanes(g)] = jnp.where(low_iota == low, 1.0, 0.0).astype(BF)
        return carry

    lax.fori_loop(0, nb, hot, 0, unroll=4)

    off_in.wait()
    halo_wait(win1, 0)
    base = (r - 1) * nb

    def product(win, g):
        picked = [win[nb + g]] + [
            win[jnp.clip(idx_ref[s, g] - base, 0, 3 * nb - 1)] for s in (1, 2, 3)
        ]
        tile = [tiles_v[g, s] for s in range(4)]
        return dot(jnp.concatenate(picked, axis=1), jnp.concatenate(tile, axis=1), NT)

    def fine_b(g, carry):
        s = scale_v[g]
        rhs = res_v[:, lanes(g)]
        v = s * rhs + s * (rhs - product(win1, g))
        x_v[g] = v
        win2[nb + g] = v.astype(BF)
        return carry

    for q in range(QUARTERS):
        lax.fori_loop(q * step, (q + 1) * step, fine_b, 0, unroll=step)
        halo_start(win2, 1, q * step, step)

    coarse_in.wait()

    def convert(c, carry):
        for k in range(2):
            at = pl.multiple_of((2 * c + k) * cdev, cdev)
            cb_v[k, c] = coarse_v[:, pl.ds(at, cdev)].astype(BF)
        return carry

    lax.fori_loop(0, nch, convert, 0, unroll=2)
    halo_wait(win2, 1)

    def residual(g, carry):
        fr_v[g] = res_v[:, lanes(g)] - product(win2, g)
        return carry

    lax.fori_loop(0, nb, residual, 0, unroll=min(32, nb))

    def restrict(c, acc):
        parts = []
        for k in range(4):
            g = 4 * c + k
            high = jnp.broadcast_to(lax.shift_right_logical(owner_row(g), 7), (cols, L))
            v = fr_v[g]
            parts.append(
                jnp.concatenate(
                    [jnp.where(high == h, v, 0.0).astype(BF) for h in range(nm)], axis=0
                )
            )
        return acc + dot(jnp.concatenate(parts, axis=1), oht[:, lanes(4 * c, 4)], NT)

    mid_rhs = lax.fori_loop(
        0, nb // 4, restrict, jnp.zeros((nm * cols, L), F32), unroll=nb // 4
    ).reshape(nm, cols, L)

    mrhs[2 : nm + 2] = mid_rhs
    rhs_edges = (
        remote(mrhs.at[pl.ds(nm, 2)], mrhs.at[pl.ds(0, 2)], msend.at[0], mrecv.at[0], {"rows": right}),
        remote(mrhs.at[pl.ds(2, 2)], mrhs.at[pl.ds(nm + 2, 2)], msend.at[1], mrecv.at[1], {"rows": left}),
    )
    for copy in rhs_edges:
        send(copy)

    def inside(v, left_side):
        keep = r > 0 if left_side else r < rows - 1
        return jnp.where(keep, v, jnp.zeros_like(v))

    def mid_product(mwin, g, before):
        v3 = jnp.concatenate([mwin[before + k] for k in range(3)], axis=1)
        t3 = jnp.concatenate([mid_v[g, k] for k in range(3)], axis=1)
        return dot(v3, t3, NT)

    mb = [None] * (nm + 2)

    def mid_b(g):
        s = ms_v[g + 1]
        rhs = mrhs[g + 1]
        mb[g] = s * rhs + s * (rhs - mid_product(mwin1, g, g))

    for g in range(2, nm + 2):
        mwin1[g] = (ms_v[g] * mrhs[g]).astype(BF)
    for g in range(2, nm):
        mid_b(g)
    for copy in edges:
        copy.wait_recv()
    for copy in rhs_edges:
        copy.wait_recv()
    for g in (0, 1, nm + 2, nm + 3):
        mwin1[g] = inside(ms_v[g] * mrhs[g], g < 2).astype(BF)
    for g in (0, 1, nm, nm + 1):
        mid_b(g)
    for g in range(nm + 2):
        v = mb[g]
        if g in (0, nm + 1):
            v = inside(v, g == 0)
        mwin2[g] = v.astype(BF)
    mid_res = [mrhs[g + 1] - mid_product(mwin2, g, g - 1) for g in range(1, nm + 1)]

    flat = jnp.concatenate(mid_res, axis=1)
    hot2 = jnp.concatenate([oh2t[1 + g] for g in range(nm)], axis=1)
    both = dot(jnp.concatenate(split(flat), axis=0), hot2, NT)
    partial = both[:cols] + both[cols:]
    even, odd = partial[:, :cdev], partial[:, cdev:]
    pair1[0] = jnp.where(core == 0, odd, even)
    swap1 = remote(pair1.at[0], pair1.at[1], psend.at[0], precv.at[0], {"rows": partner})
    send(swap1)
    swap1.wait_recv()
    coarse_rhs = jnp.where(core == 0, even, odd) + pair1[1]

    ag[core, chip] = coarse_rhs.astype(BF)

    def ag_copy(d):
        return remote(
            ag.at[core, chip], ag.at[core, chip], ags.at[0], agr.at[0],
            {"rows": 2 * lax.rem(chip + d, nch) + core},
        )

    @pl.loop(1, nch)
    def _(d):
        ag_copy(d).start()

    ag_all = remote(
        ag.at[core, pl.ds(0, nch - 1)], ag.at[core, pl.ds(0, nch - 1)],
        ags.at[0], agr.at[0], {"rows": partner},
    )
    pending.append(ag_all)
    ag_all.wait_recv()
    half = remote(ag.at[core], ag.at[core], ags.at[1], agr.at[1], {"rows": partner})
    send(half)

    def coarse_half(k, acc):
        def chunk(c, acc):
            v = jnp.concatenate([ag[k, 4 * c + i] for i in range(4)], axis=1)
            t = jnp.concatenate([cb_v[k, 4 * c + i] for i in range(4)], axis=1)
            return acc + dot(v, t, NT)

        return lax.fori_loop(0, nch // 4, chunk, acc, unroll=nch // 4)

    fix = coarse_half(core, jnp.zeros((cols, cdev), F32))
    half.wait_recv()
    fix = coarse_half(1 - core, fix)

    fx[0] = fix
    fix_out = [
        remote(fx.at[0], fx.at[1 + k], fs.at[k], fr.at[k], {"rows": to})
        for k, to in enumerate((partner, outer, outer2))
    ]
    for copy in fix_out:
        send(copy)

    def halves(a, b):
        return jnp.concatenate([jnp.where(core == 0, a, b), jnp.where(core == 0, b, a)], axis=1)

    def lifted(values, hots):
        both = dot(jnp.concatenate(split(values), axis=0), hots, NN)
        return both[:cols] + both[cols:]

    def mid_c(g, lift):
        mb[g] = mb[g] + lift
        v = mb[g]
        if g in (0, nm + 1):
            v = inside(v, g == 0)
        mwin3[g] = v.astype(BF)

    def mid_d(g):
        mb[g] = mb[g] + ms_v[g + 1] * (mrhs[g + 1] - mid_product(mwin3, g, g - 1))

    fix_out[0].wait_recv()
    pair = halves(fix, fx[1])
    lift = lifted(pair, hot2)
    for g in range(1, nm + 1):
        mid_c(g, lift[:, (g - 1) * L : g * L])
    for g in range(2, nm):
        mid_d(g)
    for copy in fix_out[1:]:
        copy.wait_recv()
    pair2 = halves(fx[3], fx[2])
    mid_c(0, lifted(jnp.where(core == 0, pair2, pair), oh2t[0]))
    mid_c(nm + 1, lifted(jnp.where(core == 0, pair, pair2), oh2t[nm + 1]))
    mid_d(1)
    mid_d(nm)

    md = jnp.concatenate(mb[1 : nm + 1], axis=0)
    cw[...] = jnp.concatenate(split(md), axis=1)

    wide = min(8, step)

    def prolong(c, carry):
        hots = oht[:, lanes(wide * c, wide)]
        up = dot(cw[...], jnp.concatenate([hots, hots], axis=0), NN)
        for k in range(wide):
            g = wide * c + k
            high = jnp.broadcast_to(lax.shift_right_logical(owner_row(g), 7), (cols, L))
            v = x_v[g]
            for h in range(nm):
                v = v + jnp.where(
                    high == h, up[h * cols : (h + 1) * cols, k * L : (k + 1) * L], 0.0
                )
            x_v[g] = v
            win3[nb + g] = v.astype(BF)
        return carry

    each = step // wide
    for q in range(QUARTERS):
        lax.fori_loop(q * each, (q + 1) * each, prolong, 0, unroll=each)
        halo_start(win3, 2, q * step, step)
    halo_wait(win3, 2)

    def finish(g, carry):
        v = x_v[g] + scale_v[g] * (res_v[:, lanes(g)] - product(win3, g))
        dir_v[:, lanes(g)] = v
        dirb[:, lanes(g)] = v.astype(BF)
        return carry

    def dir_out(q):
        at = pl.ds(q * (nb // 2) * L, (nb // 2) * L)
        return pltpu.make_async_copy(dir_v.at[:, at], dir_ref.at[:, at], dsem.at[q])

    for q in range(2):
        lax.fori_loop(q * (nb // 2), (q + 1) * (nb // 2), finish, 0, unroll=nb // 2)
        dir_out(q).start()

    basis_all.wait_recv()

    def gram(c, acc):
        t = basis_v[:, :, lanes(4 * c, 4)].reshape(nx * cols, 4 * L)
        return acc + dot(dirb[:, lanes(4 * c, 4)], t, NT)

    total = lax.fori_loop(
        0, nb // 4, gram, jnp.zeros((cols, nx * cols), F32), unroll=nb // 4
    )
    rows8 = cols // 2
    ga[core] = jnp.concatenate([total[:rows8], total[rows8:]], axis=1)
    swap3 = remote(ga.at[core], ga.at[core], gs.at[0], gr.at[0], {"rows": partner})
    send(swap3)
    swap3.wait_recv()
    gd[chip] = ga[0] + ga[1]

    @pl.loop(1, nch)
    def _(d):
        to = 2 * lax.rem(chip + d, nch) + core
        remote(gd.at[chip], gd.at[chip], gs.at[1], gr.at[1], {"rows": to}).start()

    gd_all = remote(
        gd.at[pl.ds(0, nch - 1)], gd.at[pl.ds(0, nch - 1)], gs.at[1], gr.at[1], {"rows": partner}
    )
    pending.append(gd_all)
    gd_all.wait_recv()
    parts = [gd[k] for k in range(nch)]
    while len(parts) > 1:
        parts = [a + b for a, b in zip(parts[::2], parts[1::2])]
    acc = parts[0]
    wide = nx * cols
    gram_v[...] = jnp.concatenate([acc[:, :wide], acc[:, wide:]], axis=0)
    gram_out = local(gram_v, gram_ref, 0)
    gram_out.start()
    dir_out(0).wait()
    dir_out(1).wait()
    gram_out.wait()
    pending_done()


def place(a_ref, b_ref, a_out, b_out, sem):
    copies = [
        pltpu.make_async_copy(a_ref, a_out, sem.at[0]),
        pltpu.make_async_copy(b_ref, b_out, sem.at[1]),
    ]
    for copy in copies:
        copy.start()
    for copy in copies:
        copy.wait()


def on_device(ny, nz, nx, residual, basis, fine_tiles, fine_index, mid_tiles, fine_owner, mid_owner, coarse):
    nb = fine_tiles.shape[0]
    nm = mid_tiles.shape[0]
    cols = residual.shape[1]
    cdev = coarse.shape[0]
    n = nb * L
    nch = ny * nz
    vm, dma = pltpu.VMEM, pltpu.SemaphoreType.DMA
    scratch = [
        vm((cols, n), F32), vm((nb, 4, L, L), BF), vm((nm + 2, 3, L, L), BF),
        vm((nb, L), jnp.int32), vm((nm, L), jnp.int32),
        vm(coarse.shape, F32), vm((2, nch, cdev, cdev), BF), vm((nx, cols, n), BF),
        vm((nb, cols, L), F32), vm((nb, cols, L), F32), vm((nb, cols, L), F32),
        vm((3 * nb, cols, L), BF), vm((3 * nb, cols, L), BF), vm((3 * nb, cols, L), BF),
        vm((L, n), BF), vm((nm + 2, 2 * cdev, L), BF), vm((nm + 4, cols, L), F32),
        vm((nm + 4, cols, L), F32),
        vm((nm + 4, cols, L), BF), vm((nm + 2, cols, L), BF), vm((nm + 2, cols, L), BF),
        vm((2, cols, cdev), F32), vm((4, cols, cdev), F32), vm((2, nch, cols, cdev), BF),
        vm((nm * cols, 2 * L), BF), vm((cols, n), BF),
        vm((2, cols // 2, 2 * nx * cols), F32), vm((nch, cols // 2, 2 * nx * cols), F32),
        vm((cols, n), F32), vm((cols, nx * cols), F32),
        dma((8,)), dma((QUARTERS,)), dma((3, 2)), dma((3, 2)), dma((3, 2)), dma((3, 2)),
        dma((2,)), dma((2,)), dma((1,)), dma((1,)), dma((3,)), dma((3,)),
        dma((2,)), dma((2,)), dma, dma, dma((2,)), dma((2,)),
    ]
    hbm = pl.BlockSpec(memory_space=pl.ANY)
    directions, gram = pl.pallas_call(
        functools.partial(kernel, ny, nz, nx),
        out_shape=(
            jax.ShapeDtypeStruct((cols, n), F32),
            jax.ShapeDtypeStruct((cols, nx * cols), F32),
        ),
        in_specs=[hbm, hbm, hbm, pl.BlockSpec(memory_space=pltpu.SMEM), hbm, hbm, hbm, hbm],
        out_specs=(hbm, hbm),
        scratch_shapes=scratch,
        name="vcycle",
        compiler_params=pltpu.CompilerParams(
            collective_id=0, has_side_effects=True, vmem_limit_bytes=56 * 2**20
        ),
    )(
        residual.T, basis.T, fine_tiles, fine_index.T, mid_tiles,
        fine_owner.reshape(nb, L), mid_owner.reshape(nm, L), coarse,
    )
    directions, gram = pl.pallas_call(
        place,
        out_shape=(
            jax.ShapeDtypeStruct((cols, n), F32),
            jax.ShapeDtypeStruct((cols, nx * cols), F32),
        ),
        in_specs=[hbm, hbm],
        out_specs=(hbm, hbm),
        scratch_shapes=[dma((2,))],
        name="place",
    )(directions, gram)
    return directions.T, gram.T


def solution(mesh, ny=4, nz=8):
    in_specs = (
        P("rows", "cols"),
        P("rows", "cols"),
        P("rows", None, None, None),
        P("rows", None),
        P("rows", None, None, None),
        P("rows"),
        P("rows"),
        P("rows", None),
    )
    out_specs = (P("rows", "cols"), P(None, "cols"))
    return jax.shard_map(
        functools.partial(on_device, ny, nz, mesh.shape["cols"]),
        mesh=mesh, in_specs=in_specs, out_specs=out_specs, check_vma=False,
    )
```

```python
import functools

import jax
import jax.numpy as jnp
from jax import lax
from jax.experimental import pallas as pl
from jax.experimental.pallas import tpu as pltpu
from jax.sharding import PartitionSpec as P

W = 0.6666666666666666
NT = (((1,), (1,)), ((), ()))
NN = (((1,), (0,)), ((), ()))
F32 = jnp.float32
BF = jnp.bfloat16
L = 128
QUARTERS = 4


def dot(a, b, dims):
    return lax.dot_general(a, b, dims, preferred_element_type=F32)


def split(x):
    high = x.astype(BF)
    return high, (x - high.astype(F32)).astype(BF)


def kernel(
    ny, nz, nx,
    res_hbm, basis_hbm, tiles_hbm, idx_ref, mid_hbm, own_hbm, mown_hbm, coarse_hbm,
    dir_ref, gram_ref,
    res_v, tiles_v, mid_v, own_v, mown_v, coarse_v, cb_v, basis_v, scale_v, x_v, fr_v,
    win1, win2, win3, oht, oh2t, ms_v, mrhs, mwin1, mwin2, mwin3, pair1, fx, ag, cw, dirb,
    ga, gd, dir_v, gram_v,
    lsem, dsem, hs, hr, es, er, msend, mrecv, psend, precv, fs, fr, ags, agr, bs, br, gs, gr,
):
    nb = tiles_v.shape[0]
    nm = mid_v.shape[0] - 2
    nch = ny * nz
    rows = 2 * nch
    cdev = coarse_v.shape[0]
    cols = res_v.shape[0]
    r = lax.axis_index("rows")
    x = lax.axis_index("cols")
    core = lax.rem(r, 2)
    chip = r // 2
    right = lax.rem(r + 1, rows)
    left = lax.rem(r + rows - 1, rows)
    partner = 2 * chip + 1 - core
    outer = lax.rem(r + 2 * core - 1 + rows, rows)
    outer2 = 2 * lax.rem(chip + 1 - 2 * core + nch, nch) + core
    step = nb // QUARTERS

    def remote(src, dst, ssem, rsem, where):
        return pltpu.make_async_remote_copy(
            src_ref=src, dst_ref=dst, send_sem=ssem, recv_sem=rsem,
            device_id=where, device_id_type=pl.DeviceIdType.MESH,
        )

    def local(src, dst, k):
        return pltpu.make_async_copy(src, dst, lsem.at[k])

    def lanes(g, n=1):
        return pl.ds(pl.multiple_of(g * L, L), n * L)

    pending = []

    def send(copy):
        copy.start()
        pending.append(copy)

    def pending_done():
        for copy in pending:
            copy.wait_send()

    def diag_in(q):
        at = pl.ds(q * step, step)
        return pltpu.make_async_copy(tiles_hbm.at[at, 0], tiles_v.at[at, 0], dsem.at[q])

    res_in = local(res_hbm, res_v, 1)
    off_in = local(tiles_hbm.at[:, 1:4], tiles_v.at[:, 1:4], 2)
    own_in = local(own_hbm, own_v, 3)
    mown_in = local(mown_hbm, mown_v, 4)
    mid_in = local(mid_hbm, mid_v.at[pl.ds(1, nm)], 5)
    coarse_in = local(coarse_hbm, coarse_v, 6)
    basis_in = local(basis_hbm, basis_v.at[x], 7)
    res_in.start()
    for q in range(QUARTERS):
        diag_in(q).start()
    for copy in (mid_in, own_in, mown_in, off_in, coarse_in, basis_in):
        copy.start()

    barrier = pltpu.get_barrier_semaphore()

    def greet(where):
        pl.semaphore_signal(
            barrier, inc=1, device_id=where, device_id_type=pl.DeviceIdType.MESH
        )

    greet({"rows": partner})
    greet({"rows": outer})

    @pl.loop(1, nch)
    def _(d):
        greet({"rows": 2 * lax.rem(chip + d, nch) + core})

    @pl.loop(1, nx)
    def _(d):
        greet({"cols": lax.rem(x + d, nx)})

    eye = lax.broadcasted_iota(jnp.int32, (L, L), 0) == lax.broadcasted_iota(
        jnp.int32, (L, L), 1
    )

    def weight(tile):
        d = jnp.sum(jnp.where(eye, tile.astype(F32), 0.0), axis=0, keepdims=True)
        return jnp.broadcast_to(W * (1.0 / d), (cols, L))

    def halo(win, k, lo, n):
        return (
            remote(win.at[pl.ds(nb + lo, n)], win.at[pl.ds(lo, n)], hs.at[k, 0], hr.at[k, 0], {"rows": right}),
            remote(win.at[pl.ds(nb + lo, n)], win.at[pl.ds(2 * nb + lo, n)], hs.at[k, 1], hr.at[k, 1], {"rows": left}),
        )

    def halo_start(win, k, lo, n):
        for copy in halo(win, k, lo, n):
            copy.start()
        if lo == 0:
            pending.extend(halo(win, k, 0, nb))

    def halo_wait(win, k):
        for copy in halo(win, k, 0, nb):
            copy.wait_recv()

    def first(g, carry):
        s = weight(tiles_v[g, 0])
        scale_v[g] = s
        win1[nb + g] = (s * res_v[:, lanes(g)]).astype(BF)
        return carry

    res_in.wait()
    for q in range(QUARTERS):
        diag_in(q).wait()
        lax.fori_loop(q * step, (q + 1) * step, first, 0, unroll=min(8, step))
        if q == 0:
            pl.semaphore_wait(barrier, nch - 1 + 2 + nx - 1)
        halo_start(win1, 0, q * step, step)

    basis_in.wait()

    def basis_copy(d):
        return remote(
            basis_v.at[x], basis_v.at[x], bs, br, {"cols": lax.rem(x + d, nx)}
        )

    @pl.loop(1, nx)
    def _(d):
        basis_copy(d).start()

    basis_all = remote(
        basis_v.at[pl.ds(0, nx - 1)], basis_v.at[pl.ds(0, nx - 1)], bs, br,
        {"rows": partner},
    )
    pending.append(basis_all)

    mid_in.wait()
    mown_in.wait()
    wide_iota = lax.broadcasted_iota(jnp.int32, (2 * cdev, L), 0)
    mid_base = (r - core) * cdev
    for g in range(nm):
        oh2t[1 + g] = jnp.where(
            wide_iota == mown_v[g : g + 1, :] - mid_base, 1.0, 0.0
        ).astype(BF)
        ms_v[2 + g] = weight(mid_v[1 + g, 1])
    edges = []
    for k, (buf, n, lo, hi) in enumerate(((mid_v, 1, 1, nm), (oh2t, 1, 1, nm), (ms_v, 2, 2, nm))):
        edges.append(
            remote(buf.at[pl.ds(hi, n)], buf.at[pl.ds(0, n)], es.at[k, 0], er.at[k, 0], {"rows": right})
        )
        edges.append(
            remote(buf.at[pl.ds(lo, n)], buf.at[pl.ds(lo + nm, n)], es.at[k, 1], er.at[k, 1], {"rows": left})
        )
    for copy in edges:
        send(copy)

    own_in.wait()
    low_iota = lax.broadcasted_iota(jnp.int32, (L, L), 0)
    fine_base = r * (nm * L)

    def owner_row(g):
        return own_v[pl.ds(g, 1), :] - fine_base

    def hot(g, carry):
        low = jnp.bitwise_and(owner_row(g), L - 1)
        oht[:, lanes(g)] = jnp.where(low_iota == low, 1.0, 0.0).astype(BF)
        return carry

    lax.fori_loop(0, nb, hot, 0, unroll=4)

    off_in.wait()
    halo_wait(win1, 0)
    base = (r - 1) * nb

    def product(win, g):
        picked = [win[nb + g]] + [
            win[jnp.clip(idx_ref[s, g] - base, 0, 3 * nb - 1)] for s in (1, 2, 3)
        ]
        tile = [tiles_v[g, s] for s in range(4)]
        return dot(jnp.concatenate(picked, axis=1), jnp.concatenate(tile, axis=1), NT)

    def fine_b(g, carry):
        s = scale_v[g]
        rhs = res_v[:, lanes(g)]
        v = s * rhs + s * (rhs - product(win1, g))
        x_v[g] = v
        win2[nb + g] = v.astype(BF)
        return carry

    for q in range(QUARTERS):
        lax.fori_loop(q * step, (q + 1) * step, fine_b, 0, unroll=step)
        halo_start(win2, 1, q * step, step)

    coarse_in.wait()

    def convert(c, carry):
        for k in range(2):
            at = pl.multiple_of((2 * c + k) * cdev, cdev)
            cb_v[k, c] = coarse_v[:, pl.ds(at, cdev)].astype(BF)
        return carry

    lax.fori_loop(0, nch, convert, 0, unroll=2)
    halo_wait(win2, 1)

    def residual(g, carry):
        fr_v[g] = res_v[:, lanes(g)] - product(win2, g)
        return carry

    lax.fori_loop(0, nb, residual, 0, unroll=min(32, nb))

    def restrict(c, acc):
        parts = []
        for k in range(4):
            g = 4 * c + k
            high = jnp.broadcast_to(lax.shift_right_logical(owner_row(g), 7), (cols, L))
            v = fr_v[g]
            parts.append(
                jnp.concatenate(
                    [jnp.where(high == h, v, 0.0).astype(BF) for h in range(nm)], axis=0
                )
            )
        return acc + dot(jnp.concatenate(parts, axis=1), oht[:, lanes(4 * c, 4)], NT)

    mid_rhs = lax.fori_loop(
        0, nb // 4, restrict, jnp.zeros((nm * cols, L), F32), unroll=nb // 4
    ).reshape(nm, cols, L)

    mrhs[2 : nm + 2] = mid_rhs
    rhs_edges = (
        remote(mrhs.at[pl.ds(nm, 2)], mrhs.at[pl.ds(0, 2)], msend.at[0], mrecv.at[0], {"rows": right}),
        remote(mrhs.at[pl.ds(2, 2)], mrhs.at[pl.ds(nm + 2, 2)], msend.at[1], mrecv.at[1], {"rows": left}),
    )
    for copy in rhs_edges:
        send(copy)

    def inside(v, left_side):
        keep = r > 0 if left_side else r < rows - 1
        return jnp.where(keep, v, jnp.zeros_like(v))

    def mid_product(mwin, g, before):
        v3 = jnp.concatenate([mwin[before + k] for k in range(3)], axis=1)
        t3 = jnp.concatenate([mid_v[g, k] for k in range(3)], axis=1)
        return dot(v3, t3, NT)

    mb = [None] * (nm + 2)

    def mid_b(g):
        s = ms_v[g + 1]
        rhs = mrhs[g + 1]
        mb[g] = s * rhs + s * (rhs - mid_product(mwin1, g, g))

    for g in range(2, nm + 2):
        mwin1[g] = (ms_v[g] * mrhs[g]).astype(BF)
    for g in range(2, nm):
        mid_b(g)
    for copy in edges:
        copy.wait_recv()
    for copy in rhs_edges:
        copy.wait_recv()
    for g in (0, 1, nm + 2, nm + 3):
        mwin1[g] = inside(ms_v[g] * mrhs[g], g < 2).astype(BF)
    for g in (0, 1, nm, nm + 1):
        mid_b(g)
    for g in range(nm + 2):
        v = mb[g]
        if g in (0, nm + 1):
            v = inside(v, g == 0)
        mwin2[g] = v.astype(BF)
    mid_res = [mrhs[g + 1] - mid_product(mwin2, g, g - 1) for g in range(1, nm + 1)]

    flat = jnp.concatenate(mid_res, axis=1)
    hot2 = jnp.concatenate([oh2t[1 + g] for g in range(nm)], axis=1)
    both = dot(jnp.concatenate(split(flat), axis=0), hot2, NT)
    partial = both[:cols] + both[cols:]
    even, odd = partial[:, :cdev], partial[:, cdev:]
    pair1[0] = jnp.where(core == 0, odd, even)
    swap1 = remote(pair1.at[0], pair1.at[1], psend.at[0], precv.at[0], {"rows": partner})
    send(swap1)
    swap1.wait_recv()
    coarse_rhs = jnp.where(core == 0, even, odd) + pair1[1]

    ag[core, chip] = coarse_rhs.astype(BF)

    def ag_copy(d):
        return remote(
            ag.at[core, chip], ag.at[core, chip], ags.at[0], agr.at[0],
            {"rows": 2 * lax.rem(chip + d, nch) + core},
        )

    @pl.loop(1, nch)
    def _(d):
        ag_copy(d).start()

    ag_all = remote(
        ag.at[core, pl.ds(0, nch - 1)], ag.at[core, pl.ds(0, nch - 1)],
        ags.at[0], agr.at[0], {"rows": partner},
    )
    pending.append(ag_all)
    ag_all.wait_recv()
    half = remote(ag.at[core], ag.at[core], ags.at[1], agr.at[1], {"rows": partner})
    send(half)

    def coarse_half(k, acc):
        def chunk(c, acc):
            v = jnp.concatenate([ag[k, 4 * c + i] for i in range(4)], axis=1)
            t = jnp.concatenate([cb_v[k, 4 * c + i] for i in range(4)], axis=1)
            return acc + dot(v, t, NT)

        return lax.fori_loop(0, nch // 4, chunk, acc, unroll=nch // 4)

    fix = coarse_half(core, jnp.zeros((cols, cdev), F32))
    half.wait_recv()
    fix = coarse_half(1 - core, fix)

    fx[0] = fix
    fix_out = [
        remote(fx.at[0], fx.at[1 + k], fs.at[k], fr.at[k], {"rows": to})
        for k, to in enumerate((partner, outer, outer2))
    ]
    for copy in fix_out:
        send(copy)

    def halves(a, b):
        return jnp.concatenate([jnp.where(core == 0, a, b), jnp.where(core == 0, b, a)], axis=1)

    def lifted(values, hots):
        both = dot(jnp.concatenate(split(values), axis=0), hots, NN)
        return both[:cols] + both[cols:]

    def mid_c(g, lift):
        mb[g] = mb[g] + lift
        v = mb[g]
        if g in (0, nm + 1):
            v = inside(v, g == 0)
        mwin3[g] = v.astype(BF)

    def mid_d(g):
        mb[g] = mb[g] + ms_v[g + 1] * (mrhs[g + 1] - mid_product(mwin3, g, g - 1))

    fix_out[0].wait_recv()
    pair = halves(fix, fx[1])
    lift = lifted(pair, hot2)
    for g in range(1, nm + 1):
        mid_c(g, lift[:, (g - 1) * L : g * L])
    for g in range(2, nm):
        mid_d(g)
    for copy in fix_out[1:]:
        copy.wait_recv()
    pair2 = halves(fx[3], fx[2])
    mid_c(0, lifted(jnp.where(core == 0, pair2, pair), oh2t[0]))
    mid_c(nm + 1, lifted(jnp.where(core == 0, pair, pair2), oh2t[nm + 1]))
    mid_d(1)
    mid_d(nm)

    md = jnp.concatenate(mb[1 : nm + 1], axis=0)
    cw[...] = jnp.concatenate(split(md), axis=1)

    wide = min(8, step)

    def prolong(c, carry):
        hots = oht[:, lanes(wide * c, wide)]
        up = dot(cw[...], jnp.concatenate([hots, hots], axis=0), NN)
        for k in range(wide):
            g = wide * c + k
            high = jnp.broadcast_to(lax.shift_right_logical(owner_row(g), 7), (cols, L))
            v = x_v[g]
            for h in range(nm):
                v = v + jnp.where(
                    high == h, up[h * cols : (h + 1) * cols, k * L : (k + 1) * L], 0.0
                )
            x_v[g] = v
            win3[nb + g] = v.astype(BF)
        return carry

    each = step // wide
    for q in range(QUARTERS):
        lax.fori_loop(q * each, (q + 1) * each, prolong, 0, unroll=each)
        halo_start(win3, 2, q * step, step)
    halo_wait(win3, 2)

    def finish(g, carry):
        v = x_v[g] + scale_v[g] * (res_v[:, lanes(g)] - product(win3, g))
        dir_v[:, lanes(g)] = v
        dirb[:, lanes(g)] = v.astype(BF)
        return carry

    def dir_out(q):
        at = pl.ds(q * (nb // 2) * L, (nb // 2) * L)
        return pltpu.make_async_copy(dir_v.at[:, at], dir_ref.at[:, at], dsem.at[q])

    for q in range(2):
        lax.fori_loop(q * (nb // 2), (q + 1) * (nb // 2), finish, 0, unroll=nb // 2)
        dir_out(q).start()

    basis_all.wait_recv()

    def gram(c, acc):
        t = basis_v[:, :, lanes(4 * c, 4)].reshape(nx * cols, 4 * L)
        return acc + dot(dirb[:, lanes(4 * c, 4)], t, NT)

    total = lax.fori_loop(
        0, nb // 4, gram, jnp.zeros((cols, nx * cols), F32), unroll=nb // 4
    )
    rows8 = cols // 2
    ga[core] = jnp.concatenate([total[:rows8], total[rows8:]], axis=1)
    swap3 = remote(ga.at[core], ga.at[core], gs.at[0], gr.at[0], {"rows": partner})
    send(swap3)
    swap3.wait_recv()
    gd[chip] = ga[0] + ga[1]

    @pl.loop(1, nch)
    def _(d):
        to = 2 * lax.rem(chip + d, nch) + core
        remote(gd.at[chip], gd.at[chip], gs.at[1], gr.at[1], {"rows": to}).start()

    gd_all = remote(
        gd.at[pl.ds(0, nch - 1)], gd.at[pl.ds(0, nch - 1)], gs.at[1], gr.at[1], {"rows": partner}
    )
    pending.append(gd_all)
    gd_all.wait_recv()
    parts = [gd[k] for k in range(nch)]
    while len(parts) > 1:
        parts = [a + b for a, b in zip(parts[::2], parts[1::2])]
    acc = parts[0]
    wide = nx * cols
    gram_v[...] = jnp.concatenate([acc[:, :wide], acc[:, wide:]], axis=0)
    gram_out = local(gram_v, gram_ref, 0)
    gram_out.start()
    dir_out(0).wait()
    dir_out(1).wait()
    gram_out.wait()
    pending_done()


def place(a_ref, b_ref, a_out, b_out):
    a_out[...] = a_ref[...]
    b_out[...] = b_ref[...]


def on_device(ny, nz, nx, residual, basis, fine_tiles, fine_index, mid_tiles, fine_owner, mid_owner, coarse):
    nb = fine_tiles.shape[0]
    nm = mid_tiles.shape[0]
    cols = residual.shape[1]
    cdev = coarse.shape[0]
    n = nb * L
    nch = ny * nz
    vm, dma = pltpu.VMEM, pltpu.SemaphoreType.DMA
    scratch = [
        vm((cols, n), F32), vm((nb, 4, L, L), BF), vm((nm + 2, 3, L, L), BF),
        vm((nb, L), jnp.int32), vm((nm, L), jnp.int32),
        vm(coarse.shape, F32), vm((2, nch, cdev, cdev), BF), vm((nx, cols, n), BF),
        vm((nb, cols, L), F32), vm((nb, cols, L), F32), vm((nb, cols, L), F32),
        vm((3 * nb, cols, L), BF), vm((3 * nb, cols, L), BF), vm((3 * nb, cols, L), BF),
        vm((L, n), BF), vm((nm + 2, 2 * cdev, L), BF), vm((nm + 4, cols, L), F32),
        vm((nm + 4, cols, L), F32),
        vm((nm + 4, cols, L), BF), vm((nm + 2, cols, L), BF), vm((nm + 2, cols, L), BF),
        vm((2, cols, cdev), F32), vm((4, cols, cdev), F32), vm((2, nch, cols, cdev), BF),
        vm((nm * cols, 2 * L), BF), vm((cols, n), BF),
        vm((2, cols // 2, 2 * nx * cols), F32), vm((nch, cols // 2, 2 * nx * cols), F32),
        vm((cols, n), F32), vm((cols, nx * cols), F32),
        dma((8,)), dma((QUARTERS,)), dma((3, 2)), dma((3, 2)), dma((3, 2)), dma((3, 2)),
        dma((2,)), dma((2,)), dma((1,)), dma((1,)), dma((3,)), dma((3,)),
        dma((2,)), dma((2,)), dma, dma, dma((2,)), dma((2,)),
    ]
    hbm = pl.BlockSpec(memory_space=pl.ANY)
    directions, gram = pl.pallas_call(
        functools.partial(kernel, ny, nz, nx),
        out_shape=(
            jax.ShapeDtypeStruct((cols, n), F32),
            jax.ShapeDtypeStruct((cols, nx * cols), F32),
        ),
        in_specs=[hbm, hbm, hbm, pl.BlockSpec(memory_space=pltpu.SMEM), hbm, hbm, hbm, hbm],
        out_specs=(hbm, hbm),
        scratch_shapes=scratch,
        name="vcycle",
        compiler_params=pltpu.CompilerParams(
            collective_id=0, has_side_effects=True, vmem_limit_bytes=56 * 2**20
        ),
    )(
        residual.T, basis.T, fine_tiles, fine_index.T, mid_tiles,
        fine_owner.reshape(nb, L), mid_owner.reshape(nm, L), coarse,
    )
    directions, gram = pl.pallas_call(
        place,
        out_shape=(
            jax.ShapeDtypeStruct((cols, n), F32),
            jax.ShapeDtypeStruct((cols, nx * cols), F32),
        ),
        grid=(2,),
        in_specs=[pl.BlockSpec((cols, n // 2), lambda i: (0, i)), pl.BlockSpec((cols, nx * cols), lambda i: (0, 0))],
        out_specs=(pl.BlockSpec((cols, n // 2), lambda i: (0, i)), pl.BlockSpec((cols, nx * cols), lambda i: (0, 0))),
        name="place",
    )(directions, gram)
    return directions.T, gram.T


def solution(mesh, ny=4, nz=8):
    in_specs = (
        P("rows", "cols"),
        P("rows", "cols"),
        P("rows", None, None, None),
        P("rows", None),
        P("rows", None, None, None),
        P("rows"),
        P("rows"),
        P("rows", None),
    )
    out_specs = (P("rows", "cols"), P(None, "cols"))
    return jax.shard_map(
        functools.partial(on_device, ny, nz, mesh.shape["cols"]),
        mesh=mesh, in_specs=in_specs, out_specs=out_specs, check_vma=False,
    )
```

```python
import functools

import jax
import jax.numpy as jnp
from jax import lax
from jax.experimental import pallas as pl
from jax.experimental.pallas import tpu as pltpu
from jax.sharding import PartitionSpec as P

W = 0.6666666666666666
NT = (((1,), (1,)), ((), ()))
NN = (((1,), (0,)), ((), ()))
F32 = jnp.float32
BF = jnp.bfloat16
L = 128
QUARTERS = 4


def dot(a, b, dims):
    return lax.dot_general(a, b, dims, preferred_element_type=F32)


def split(x):
    high = x.astype(BF)
    return high, (x - high.astype(F32)).astype(BF)


def kernel(
    ny, nz, nx,
    res_hbm, basis_hbm, tiles_hbm, idx_ref, mid_hbm, own_hbm, mown_hbm, coarse_hbm,
    dir_ref, gram_ref,
    res_v, tiles_v, mid_v, own_v, mown_v, coarse_v, cb_v, basis_v, scale_v, x_v, fr_v,
    win1, win2, win3, oht, oh2t, ms_v, mrhs, mwin1, mwin2, mwin3, pair1, fx, ag, cw, dirb,
    ga, gd, dir_v, gram_v,
    lsem, dsem, hs, hr, es, er, msend, mrecv, psend, precv, fs, fr, ags, agr, bs, br, gs, gr,
):
    nb = tiles_v.shape[0]
    nm = mid_v.shape[0] - 2
    nch = ny * nz
    rows = 2 * nch
    cdev = coarse_v.shape[0]
    cols = res_v.shape[0]
    r = lax.axis_index("rows")
    x = lax.axis_index("cols")
    core = lax.rem(r, 2)
    chip = r // 2
    partner = 2 * chip + 1 - core
    outer = lax.rem(r + 2 * core - 1 + rows, rows)
    outer2 = 2 * lax.rem(chip + 1 - 2 * core + nch, nch) + core
    step = nb // QUARTERS

    def remote(src, dst, ssem, rsem, where):
        return pltpu.make_async_remote_copy(
            src_ref=src, dst_ref=dst, send_sem=ssem, recv_sem=rsem,
            device_id=where, device_id_type=pl.DeviceIdType.MESH,
        )

    def local(src, dst, k):
        return pltpu.make_async_copy(src, dst, lsem.at[k])

    def lanes(g, n=1):
        return pl.ds(pl.multiple_of(g * L, L), n * L)

    pending = []
    bordered = jnp.logical_and(r > 0, r < rows - 1)

    def guarded(when, act):
        if when is None:
            act()
        else:
            pl.when(when)(act)

    def send(copy, when=None):
        guarded(when, copy.start)
        pending.append((copy, when))

    def received(copy, when=None):
        guarded(when, copy.wait_recv)

    def pending_done():
        for copy, when in pending:
            guarded(when, copy.wait_send)

    def diag_in(q):
        at = pl.ds(q * step, step)
        return pltpu.make_async_copy(tiles_hbm.at[at, 0], tiles_v.at[at, 0], dsem.at[q])

    res_in = local(res_hbm, res_v, 1)
    off_in = local(tiles_hbm.at[:, 1:4], tiles_v.at[:, 1:4], 2)
    own_in = local(own_hbm, own_v, 3)
    mown_in = local(mown_hbm, mown_v, 4)
    mid_in = local(mid_hbm, mid_v.at[pl.ds(1, nm)], 5)
    coarse_in = local(coarse_hbm, coarse_v, 6)
    basis_in = local(basis_hbm, basis_v.at[x], 7)
    res_in.start()
    for q in range(QUARTERS):
        diag_in(q).start()
    for copy in (mid_in, own_in, mown_in, off_in, coarse_in, basis_in):
        copy.start()

    barrier = pltpu.get_barrier_semaphore()

    def greet(where):
        pl.semaphore_signal(
            barrier, inc=1, device_id=where, device_id_type=pl.DeviceIdType.MESH
        )

    greet({"rows": partner})
    greet({"rows": outer})

    @pl.loop(1, nch)
    def _(d):
        greet({"rows": 2 * lax.rem(chip + d, nch) + core})

    @pl.loop(1, nx)
    def _(d):
        greet({"cols": lax.rem(x + d, nx)})

    eye = lax.broadcasted_iota(jnp.int32, (L, L), 0) == lax.broadcasted_iota(
        jnp.int32, (L, L), 1
    )

    def weight(tile):
        d = jnp.sum(jnp.where(eye, tile.astype(F32), 0.0), axis=0, keepdims=True)
        return jnp.broadcast_to(W * (1.0 / d), (cols, L))

    far_part = 2 * nb * (1 - core)
    near_part = 2 * nb * core

    def halo(win, k, lo, n):
        own = win.at[pl.ds(nb + lo, n)]
        return (
            (remote(own, win.at[pl.ds(far_part + lo, n)], hs.at[k, 0], hr.at[k, 0], {"rows": outer}), bordered),
            (remote(own, win.at[pl.ds(near_part + lo, n)], hs.at[k, 1], hr.at[k, 1], {"rows": partner}), None),
        )

    def halo_start(win, k, lo, n):
        for copy, when in halo(win, k, lo, n):
            guarded(when, copy.start)
        if lo == 0:
            pending.extend(halo(win, k, 0, nb))

    def halo_wait(win, k):
        for copy, when in halo(win, k, 0, nb):
            received(copy, when)

    yc = chip // nz
    zc = lax.rem(chip, nz)
    steps = sorted(
        ((dy, dz) for dy in range(ny) for dz in range(nz) if dy or dz),
        key=lambda d: -min(d[0], ny - d[0]) - min(d[1], nz - d[1]),
    )

    def chip_at(dy, dz):
        return lax.rem(yc + dy, ny) * nz + lax.rem(zc + dz, nz)

    def first(g, carry):
        s = weight(tiles_v[g, 0])
        scale_v[g] = s
        win1[nb + g] = (s * res_v[:, lanes(g)]).astype(BF)
        return carry

    res_in.wait()
    for q in range(QUARTERS):
        diag_in(q).wait()
        lax.fori_loop(q * step, (q + 1) * step, first, 0, unroll=min(8, step))
        if q == 0:
            pl.semaphore_wait(barrier, nch - 1 + 2 + nx - 1)
        halo_start(win1, 0, q * step, step)

    basis_in.wait()

    def basis_copy(d):
        return remote(
            basis_v.at[x], basis_v.at[x], bs, br, {"cols": lax.rem(x + d, nx)}
        )

    @pl.loop(1, nx)
    def _(d):
        basis_copy(d).start()

    basis_all = remote(
        basis_v.at[pl.ds(0, nx - 1)], basis_v.at[pl.ds(0, nx - 1)], bs, br,
        {"rows": partner},
    )
    pending.append((basis_all, None))

    mid_in.wait()
    mown_in.wait()
    wide_iota = lax.broadcasted_iota(jnp.int32, (2 * cdev, L), 0)
    mid_base = (r - core) * cdev
    for g in range(nm):
        oh2t[1 + g] = jnp.where(
            wide_iota == mown_v[g : g + 1, :] - mid_base, 1.0, 0.0
        ).astype(BF)
        ms_v[2 + g] = weight(mid_v[1 + g, 1])

    def edge_copies(buf, n, own, ssem, rsem):
        out_at = own + core * (nm - n)
        out_to = own + nm - core * (nm + n)
        in_at = own + (1 - core) * (nm - n)
        in_to = own - n + core * (nm + n)
        return (
            (remote(buf.at[pl.ds(out_at, n)], buf.at[pl.ds(out_to, n)], ssem.at[0], rsem.at[0], {"rows": outer}), bordered),
            (remote(buf.at[pl.ds(in_at, n)], buf.at[pl.ds(in_to, n)], ssem.at[1], rsem.at[1], {"rows": partner}), None),
        )

    edges = []
    for k, (buf, n, own) in enumerate(((mid_v, 1, 1), (oh2t, 1, 1), (ms_v, 2, 2))):
        edges.extend(edge_copies(buf, n, own, es.at[k], er.at[k]))
    for copy, when in edges:
        send(copy, when)

    own_in.wait()
    low_iota = lax.broadcasted_iota(jnp.int32, (L, L), 0)
    fine_base = r * (nm * L)

    def owner_row(g):
        return own_v[pl.ds(g, 1), :] - fine_base

    def hot(g, carry):
        low = jnp.bitwise_and(owner_row(g), L - 1)
        oht[:, lanes(g)] = jnp.where(low_iota == low, 1.0, 0.0).astype(BF)
        return carry

    lax.fori_loop(0, nb, hot, 0, unroll=4)

    off_in.wait()
    halo_wait(win1, 0)
    base = (r - 1) * nb

    def product(win, g):
        picked = [win[nb + g]] + [
            win[jnp.clip(idx_ref[s, g] - base, 0, 3 * nb - 1)] for s in (1, 2, 3)
        ]
        tile = [tiles_v[g, s] for s in range(4)]
        return dot(jnp.concatenate(picked, axis=1), jnp.concatenate(tile, axis=1), NT)

    def fine_b(g, carry):
        s = scale_v[g]
        rhs = res_v[:, lanes(g)]
        v = s * rhs + s * (rhs - product(win1, g))
        x_v[g] = v
        win2[nb + g] = v.astype(BF)
        return carry

    for q in range(QUARTERS):
        lax.fori_loop(q * step, (q + 1) * step, fine_b, 0, unroll=step)
        halo_start(win2, 1, q * step, step)

    coarse_in.wait()

    def convert(c, carry):
        for k in range(2):
            at = pl.multiple_of((2 * c + k) * cdev, cdev)
            cb_v[k, c] = coarse_v[:, pl.ds(at, cdev)].astype(BF)
        return carry

    lax.fori_loop(0, nch, convert, 0, unroll=2)
    halo_wait(win2, 1)

    def residual(g, carry):
        fr_v[g] = res_v[:, lanes(g)] - product(win2, g)
        return carry

    lax.fori_loop(0, nb, residual, 0, unroll=min(32, nb))

    def restrict(c, acc):
        parts = []
        for k in range(4):
            g = 4 * c + k
            high = jnp.broadcast_to(lax.shift_right_logical(owner_row(g), 7), (cols, L))
            v = fr_v[g]
            parts.append(
                jnp.concatenate(
                    [jnp.where(high == h, v, 0.0).astype(BF) for h in range(nm)], axis=0
                )
            )
        return acc + dot(jnp.concatenate(parts, axis=1), oht[:, lanes(4 * c, 4)], NT)

    mid_rhs = lax.fori_loop(
        0, nb // 4, restrict, jnp.zeros((nm * cols, L), F32), unroll=nb // 4
    ).reshape(nm, cols, L)

    mrhs[2 : nm + 2] = mid_rhs
    rhs_edges = edge_copies(mrhs, 2, 2, msend, mrecv)
    for copy, when in rhs_edges:
        send(copy, when)

    def inside(v, left_side):
        keep = r > 0 if left_side else r < rows - 1
        return jnp.where(keep, v, jnp.zeros_like(v))

    def mid_product(mwin, g, before):
        v3 = jnp.concatenate([mwin[before + k] for k in range(3)], axis=1)
        t3 = jnp.concatenate([mid_v[g, k] for k in range(3)], axis=1)
        return dot(v3, t3, NT)

    mb = [None] * (nm + 2)

    def mid_b(g):
        s = ms_v[g + 1]
        rhs = mrhs[g + 1]
        mb[g] = s * rhs + s * (rhs - mid_product(mwin1, g, g))

    for g in range(2, nm + 2):
        mwin1[g] = (ms_v[g] * mrhs[g]).astype(BF)
    for g in range(2, nm):
        mid_b(g)
    for copy, when in (*edges, *rhs_edges):
        received(copy, when)
    for g in (0, 1, nm + 2, nm + 3):
        mwin1[g] = inside(ms_v[g] * mrhs[g], g < 2).astype(BF)
    for g in (0, 1, nm, nm + 1):
        mid_b(g)
    for g in range(nm + 2):
        v = mb[g]
        if g in (0, nm + 1):
            v = inside(v, g == 0)
        mwin2[g] = v.astype(BF)
    mid_res = [mrhs[g + 1] - mid_product(mwin2, g, g - 1) for g in range(1, nm + 1)]

    flat = jnp.concatenate(mid_res, axis=1)
    hot2 = jnp.concatenate([oh2t[1 + g] for g in range(nm)], axis=1)
    both = dot(jnp.concatenate(split(flat), axis=0), hot2, NT)
    partial = both[:cols] + both[cols:]
    even, odd = partial[:, :cdev], partial[:, cdev:]
    pair1[0] = jnp.where(core == 0, odd, even)
    swap1 = remote(pair1.at[0], pair1.at[1], psend.at[0], precv.at[0], {"rows": partner})
    send(swap1)
    swap1.wait_recv()
    coarse_rhs = jnp.where(core == 0, even, odd) + pair1[1]

    ag[core, chip] = coarse_rhs.astype(BF)

    for d in steps:
        to = 2 * chip_at(*d) + core
        remote(ag.at[core, chip], ag.at[core, chip], ags.at[0], agr.at[0], {"rows": to}).start()

    ag_all = remote(
        ag.at[core, pl.ds(0, nch - 1)], ag.at[core, pl.ds(0, nch - 1)],
        ags.at[0], agr.at[0], {"rows": partner},
    )
    pending.append((ag_all, None))
    ag_all.wait_recv()
    half = remote(ag.at[core], ag.at[core], ags.at[1], agr.at[1], {"rows": partner})
    send(half)

    def coarse_half(k, acc):
        def chunk(c, acc):
            v = jnp.concatenate([ag[k, 4 * c + i] for i in range(4)], axis=1)
            t = jnp.concatenate([cb_v[k, 4 * c + i] for i in range(4)], axis=1)
            return acc + dot(v, t, NT)

        return lax.fori_loop(0, nch // 4, chunk, acc, unroll=nch // 4)

    fix = coarse_half(core, jnp.zeros((cols, cdev), F32))
    half.wait_recv()
    fix = coarse_half(1 - core, fix)

    fx[0] = fix
    fix_out = [
        remote(fx.at[0], fx.at[1 + k], fs.at[k], fr.at[k], {"rows": to})
        for k, to in enumerate((partner, outer, outer2))
    ]
    last_but = jnp.logical_and(r != 1, r != rows - 2)
    for copy, when in zip(fix_out[::-1], (last_but, bordered, None)):
        send(copy, when)

    def halves(a, b):
        return jnp.concatenate([jnp.where(core == 0, a, b), jnp.where(core == 0, b, a)], axis=1)

    def lifted(values, hots):
        both = dot(jnp.concatenate(split(values), axis=0), hots, NN)
        return both[:cols] + both[cols:]

    def mid_c(g, lift):
        mb[g] = mb[g] + lift
        v = mb[g]
        if g in (0, nm + 1):
            v = inside(v, g == 0)
        mwin3[g] = v.astype(BF)

    def mid_d(g):
        mb[g] = mb[g] + ms_v[g + 1] * (mrhs[g + 1] - mid_product(mwin3, g, g - 1))

    fix_out[0].wait_recv()
    pair = halves(fix, fx[1])
    lift = lifted(pair, hot2)
    for g in range(1, nm + 1):
        mid_c(g, lift[:, (g - 1) * L : g * L])
    for g in range(2, nm):
        mid_d(g)
    for copy in fix_out[1:]:
        received(copy, bordered)
    pair2 = halves(fx[3], fx[2])
    mid_c(0, lifted(jnp.where(core == 0, pair2, pair), oh2t[0]))
    mid_c(nm + 1, lifted(jnp.where(core == 0, pair, pair2), oh2t[nm + 1]))
    mid_d(1)
    mid_d(nm)

    md = jnp.concatenate(mb[1 : nm + 1], axis=0)
    cw[...] = jnp.concatenate(split(md), axis=1)

    wide = min(8, step)

    def prolong(c, carry):
        hots = oht[:, lanes(wide * c, wide)]
        up = dot(cw[...], jnp.concatenate([hots, hots], axis=0), NN)
        for k in range(wide):
            g = wide * c + k
            high = jnp.broadcast_to(lax.shift_right_logical(owner_row(g), 7), (cols, L))
            v = x_v[g]
            for h in range(nm):
                v = v + jnp.where(
                    high == h, up[h * cols : (h + 1) * cols, k * L : (k + 1) * L], 0.0
                )
            x_v[g] = v
            win3[nb + g] = v.astype(BF)
        return carry

    each = step // wide
    for q in range(QUARTERS):
        lax.fori_loop(q * each, (q + 1) * each, prolong, 0, unroll=each)
        halo_start(win3, 2, q * step, step)
    halo_wait(win3, 2)

    def finish(g, carry):
        v = x_v[g] + scale_v[g] * (res_v[:, lanes(g)] - product(win3, g))
        dir_v[:, lanes(g)] = v
        dirb[:, lanes(g)] = v.astype(BF)
        return carry

    def dir_out(q):
        at = pl.ds(q * (nb // 2) * L, (nb // 2) * L)
        return pltpu.make_async_copy(dir_v.at[:, at], dir_ref.at[:, at], dsem.at[q])

    for q in range(2):
        lax.fori_loop(q * (nb // 2), (q + 1) * (nb // 2), finish, 0, unroll=nb // 2)
        dir_out(q).start()

    basis_all.wait_recv()

    def gram(c, acc):
        t = basis_v[:, :, lanes(4 * c, 4)].reshape(nx * cols, 4 * L)
        return acc + dot(dirb[:, lanes(4 * c, 4)], t, NT)

    total = lax.fori_loop(
        0, nb // 4, gram, jnp.zeros((cols, nx * cols), F32), unroll=nb // 4
    )
    rows8 = cols // 2
    ga[core] = jnp.concatenate([total[:rows8], total[rows8:]], axis=1)
    swap3 = remote(ga.at[core], ga.at[core], gs.at[0], gr.at[0], {"rows": partner})
    send(swap3)
    swap3.wait_recv()
    gd[chip] = ga[0] + ga[1]

    for d in steps:
        to = 2 * chip_at(*d) + core
        remote(gd.at[chip], gd.at[chip], gs.at[1], gr.at[1], {"rows": to}).start()

    gd_all = remote(
        gd.at[pl.ds(0, nch - 1)], gd.at[pl.ds(0, nch - 1)], gs.at[1], gr.at[1], {"rows": partner}
    )
    pending.append((gd_all, None))
    gd_all.wait_recv()
    parts = [gd[k] for k in range(nch)]
    while len(parts) > 1:
        parts = [a + b for a, b in zip(parts[::2], parts[1::2])]
    acc = parts[0]
    wide = nx * cols
    gram_v[...] = jnp.concatenate([acc[:, :wide], acc[:, wide:]], axis=0)
    gram_out = local(gram_v, gram_ref, 0)
    gram_out.start()
    dir_out(0).wait()
    dir_out(1).wait()
    gram_out.wait()
    pending_done()


def place(a_ref, b_ref, a_out, b_out):
    a_out[...] = a_ref[...]
    b_out[...] = b_ref[...]


def on_device(ny, nz, nx, residual, basis, fine_tiles, fine_index, mid_tiles, fine_owner, mid_owner, coarse):
    nb = fine_tiles.shape[0]
    nm = mid_tiles.shape[0]
    cols = residual.shape[1]
    cdev = coarse.shape[0]
    n = nb * L
    nch = ny * nz
    vm, dma = pltpu.VMEM, pltpu.SemaphoreType.DMA
    scratch = [
        vm((cols, n), F32), vm((nb, 4, L, L), BF), vm((nm + 2, 3, L, L), BF),
        vm((nb, L), jnp.int32), vm((nm, L), jnp.int32),
        vm(coarse.shape, F32), vm((2, nch, cdev, cdev), BF), vm((nx, cols, n), BF),
        vm((nb, cols, L), F32), vm((nb, cols, L), F32), vm((nb, cols, L), F32),
        vm((3 * nb, cols, L), BF), vm((3 * nb, cols, L), BF), vm((3 * nb, cols, L), BF),
        vm((L, n), BF), vm((nm + 2, 2 * cdev, L), BF), vm((nm + 4, cols, L), F32),
        vm((nm + 4, cols, L), F32),
        vm((nm + 4, cols, L), BF), vm((nm + 2, cols, L), BF), vm((nm + 2, cols, L), BF),
        vm((2, cols, cdev), F32), vm((4, cols, cdev), F32), vm((2, nch, cols, cdev), BF),
        vm((nm * cols, 2 * L), BF), vm((cols, n), BF),
        vm((2, cols // 2, 2 * nx * cols), F32), vm((nch, cols // 2, 2 * nx * cols), F32),
        vm((cols, n), F32), vm((cols, nx * cols), F32),
        dma((8,)), dma((QUARTERS,)), dma((3, 2)), dma((3, 2)), dma((3, 2)), dma((3, 2)),
        dma((2,)), dma((2,)), dma((1,)), dma((1,)), dma((3,)), dma((3,)),
        dma((2,)), dma((2,)), dma, dma, dma((2,)), dma((2,)),
    ]
    hbm = pl.BlockSpec(memory_space=pl.ANY)
    directions, gram = pl.pallas_call(
        functools.partial(kernel, ny, nz, nx),
        out_shape=(
            jax.ShapeDtypeStruct((cols, n), F32),
            jax.ShapeDtypeStruct((cols, nx * cols), F32),
        ),
        in_specs=[hbm, hbm, hbm, pl.BlockSpec(memory_space=pltpu.SMEM), hbm, hbm, hbm, hbm],
        out_specs=(hbm, hbm),
        scratch_shapes=scratch,
        name="vcycle",
        compiler_params=pltpu.CompilerParams(
            collective_id=0, has_side_effects=True, vmem_limit_bytes=56 * 2**20
        ),
    )(
        residual.T, basis.T, fine_tiles, fine_index.T, mid_tiles,
        fine_owner.reshape(nb, L), mid_owner.reshape(nm, L), coarse,
    )
    directions, gram = pl.pallas_call(
        place,
        out_shape=(
            jax.ShapeDtypeStruct((cols, n), F32),
            jax.ShapeDtypeStruct((cols, nx * cols), F32),
        ),
        grid=(2,),
        in_specs=[pl.BlockSpec((cols, n // 2), lambda i: (0, i)), pl.BlockSpec((cols, nx * cols), lambda i: (0, 0))],
        out_specs=(pl.BlockSpec((cols, n // 2), lambda i: (0, i)), pl.BlockSpec((cols, nx * cols), lambda i: (0, 0))),
        name="place",
    )(directions, gram)
    return directions.T, gram.T


def solution(mesh, ny=4, nz=8):
    in_specs = (
        P("rows", "cols"),
        P("rows", "cols"),
        P("rows", None, None, None),
        P("rows", None),
        P("rows", None, None, None),
        P("rows"),
        P("rows"),
        P("rows", None),
    )
    out_specs = (P("rows", "cols"), P(None, "cols"))
    return jax.shard_map(
        functools.partial(on_device, ny, nz, mesh.shape["cols"]),
        mesh=mesh, in_specs=in_specs, out_specs=out_specs, check_vma=False,
    )
```

```python
import functools

import jax
import jax.numpy as jnp
from jax import lax
from jax.experimental import pallas as pl
from jax.experimental.pallas import tpu as pltpu
from jax.sharding import PartitionSpec as P

W = 0.6666666666666666
NT = (((1,), (1,)), ((), ()))
NN = (((1,), (0,)), ((), ()))
F32 = jnp.float32
BF = jnp.bfloat16
L = 128
QUARTERS = 4


def dot(a, b, dims):
    return lax.dot_general(a, b, dims, preferred_element_type=F32)


def split(x):
    high = x.astype(BF)
    return high, (x - high.astype(F32)).astype(BF)


def kernel(
    ny, nz, nx,
    res_hbm, basis_hbm, tiles_hbm, idx_ref, mid_hbm, own_hbm, mown_hbm, coarse_hbm,
    dir_ref, gram_ref,
    res_v, tiles_v, mid_v, own_v, mown_v, coarse_v, cb_v, basis_v, scale_v, x_v, fr_v,
    win1, win2, win3, oht, oh2t, ms_v, mrhs, mwin1, mwin2, mwin3, pair1, fx, ag, cw, dirb,
    ga, gd, dir_v, gram_v,
    lsem, dsem, hs, hr, es, er, msend, mrecv, psend, precv, fs, fr, ags, agr, bs, br, gs, gr,
):
    nb = tiles_v.shape[0]
    nm = mid_v.shape[0] - 2
    nch = ny * nz
    rows = 2 * nch
    cdev = coarse_v.shape[0]
    cols = res_v.shape[0]
    r = lax.axis_index("rows")
    x = lax.axis_index("cols")
    core = lax.rem(r, 2)
    chip = r // 2
    partner = 2 * chip + 1 - core
    outer = lax.rem(r + 2 * core - 1 + rows, rows)
    outer2 = 2 * lax.rem(chip + 1 - 2 * core + nch, nch) + core
    step = nb // QUARTERS

    def remote(src, dst, ssem, rsem, where):
        return pltpu.make_async_remote_copy(
            src_ref=src, dst_ref=dst, send_sem=ssem, recv_sem=rsem,
            device_id=where, device_id_type=pl.DeviceIdType.MESH,
        )

    def local(src, dst, k):
        return pltpu.make_async_copy(src, dst, lsem.at[k])

    def lanes(g, n=1):
        return pl.ds(pl.multiple_of(g * L, L), n * L)

    pending = []
    bordered = jnp.logical_and(r > 0, r < rows - 1)

    def guarded(when, act):
        if when is None:
            act()
        else:
            pl.when(when)(act)

    def send(copy, when=None):
        guarded(when, copy.start)
        pending.append((copy, when))

    def received(copy, when=None):
        guarded(when, copy.wait_recv)

    def pending_done():
        for copy, when in pending:
            guarded(when, copy.wait_send)

    def diag_in(q):
        at = pl.ds(q * step, step)
        return pltpu.make_async_copy(tiles_hbm.at[at, 0], tiles_v.at[at, 0], dsem.at[q])

    res_in = local(res_hbm, res_v, 1)
    off_in = local(tiles_hbm.at[:, 1:4], tiles_v.at[:, 1:4], 2)
    own_in = local(own_hbm, own_v, 3)
    mown_in = local(mown_hbm, mown_v, 4)
    mid_in = local(mid_hbm, mid_v.at[pl.ds(1, nm)], 5)
    coarse_in = local(coarse_hbm, coarse_v, 6)
    basis_in = local(basis_hbm, basis_v.at[x], 7)
    barrier = pltpu.get_barrier_semaphore()

    def greet(where):
        pl.semaphore_signal(
            barrier, inc=1, device_id=where, device_id_type=pl.DeviceIdType.MESH
        )

    greet({"rows": partner})
    greet({"rows": outer})

    @pl.loop(1, nch)
    def _(d):
        greet({"rows": 2 * lax.rem(chip + d, nch) + core})

    @pl.loop(1, nx)
    def _(d):
        greet({"cols": lax.rem(x + d, nx)})

    res_in.start()
    for q in range(QUARTERS):
        diag_in(q).start()
    for copy in (mid_in, own_in, mown_in, off_in, coarse_in, basis_in):
        copy.start()

    eye = lax.broadcasted_iota(jnp.int32, (L, L), 0) == lax.broadcasted_iota(
        jnp.int32, (L, L), 1
    )

    def weight(tile):
        d = jnp.sum(jnp.where(eye, tile.astype(F32), 0.0), axis=0, keepdims=True)
        return jnp.broadcast_to(W * (1.0 / d), (cols, L))

    far_part = 2 * nb * (1 - core)
    near_part = 2 * nb * core

    def halo(win, k, lo, n):
        own = win.at[pl.ds(nb + lo, n)]
        return (
            (remote(own, win.at[pl.ds(far_part + lo, n)], hs.at[k, 0], hr.at[k, 0], {"rows": outer}), bordered),
            (remote(own, win.at[pl.ds(near_part + lo, n)], hs.at[k, 1], hr.at[k, 1], {"rows": partner}), None),
        )

    def halo_start(win, k, lo, n):
        for copy, when in halo(win, k, lo, n):
            guarded(when, copy.start)
        if lo == 0:
            pending.extend(halo(win, k, 0, nb))

    def halo_wait(win, k):
        for copy, when in halo(win, k, 0, nb):
            received(copy, when)

    yc = chip // nz
    zc = lax.rem(chip, nz)
    steps = sorted(
        ((dy, dz) for dy in range(ny) for dz in range(nz) if dy or dz),
        key=lambda d: -min(d[0], ny - d[0]) - min(d[1], nz - d[1]),
    )

    def chip_at(dy, dz):
        return lax.rem(yc + dy, ny) * nz + lax.rem(zc + dz, nz)

    def first(g, carry):
        s = weight(tiles_v[g, 0])
        scale_v[g] = s
        win1[nb + g] = (s * res_v[:, lanes(g)]).astype(BF)
        return carry

    res_in.wait()
    for q in range(QUARTERS):
        diag_in(q).wait()
        lax.fori_loop(q * step, (q + 1) * step, first, 0, unroll=min(8, step))
        if q == 0:
            pl.semaphore_wait(barrier, nch - 1 + 2 + nx - 1)
        halo_start(win1, 0, q * step, step)

    basis_in.wait()

    def basis_copy(d):
        return remote(
            basis_v.at[x], basis_v.at[x], bs, br, {"cols": lax.rem(x + d, nx)}
        )

    @pl.loop(1, nx)
    def _(d):
        basis_copy(d).start()

    basis_all = remote(
        basis_v.at[pl.ds(0, nx - 1)], basis_v.at[pl.ds(0, nx - 1)], bs, br,
        {"rows": partner},
    )
    pending.append((basis_all, None))

    mid_in.wait()
    mown_in.wait()
    wide_iota = lax.broadcasted_iota(jnp.int32, (2 * cdev, L), 0)
    mid_base = (r - core) * cdev
    for g in range(nm):
        oh2t[1 + g] = jnp.where(
            wide_iota == mown_v[g : g + 1, :] - mid_base, 1.0, 0.0
        ).astype(BF)
        ms_v[2 + g] = weight(mid_v[1 + g, 1])
        for k in range(3):
            mid_v[1 + g, k] = mid_v[1 + g, k].T

    def edge_copies(buf, n, own, ssem, rsem):
        out_at = own + core * (nm - n)
        out_to = own + nm - core * (nm + n)
        in_at = own + (1 - core) * (nm - n)
        in_to = own - n + core * (nm + n)
        return (
            (remote(buf.at[pl.ds(out_at, n)], buf.at[pl.ds(out_to, n)], ssem.at[0], rsem.at[0], {"rows": outer}), bordered),
            (remote(buf.at[pl.ds(in_at, n)], buf.at[pl.ds(in_to, n)], ssem.at[1], rsem.at[1], {"rows": partner}), None),
        )

    edges = []
    for k, (buf, n, own) in enumerate(((mid_v, 1, 1), (oh2t, 1, 1), (ms_v, 2, 2))):
        edges.extend(edge_copies(buf, n, own, es.at[k], er.at[k]))
    for copy, when in edges:
        send(copy, when)

    own_in.wait()
    low_iota = lax.broadcasted_iota(jnp.int32, (L, L), 0)
    fine_base = r * (nm * L)

    def owner_row(g):
        return own_v[pl.ds(g, 1), :] - fine_base

    def hot(g, carry):
        low = jnp.bitwise_and(owner_row(g), L - 1)
        oht[:, lanes(g)] = jnp.where(low_iota == low, 1.0, 0.0).astype(BF)
        return carry

    lax.fori_loop(0, nb, hot, 0, unroll=4)

    off_in.wait()

    def turn(g, carry):
        for s in range(4):
            tiles_v[g, s] = tiles_v[g, s].T
        return carry

    lax.fori_loop(0, nb, turn, 0, unroll=min(16, nb))
    halo_wait(win1, 0)
    base = (r - 1) * nb

    def product(win, g):
        picked = [win[nb + g]] + [
            win[jnp.clip(idx_ref[s, g] - base, 0, 3 * nb - 1)] for s in (1, 2, 3)
        ]
        tile = [tiles_v[g, s] for s in range(4)]
        return dot(jnp.concatenate(picked, axis=1), jnp.concatenate(tile, axis=0), NN)

    def fine_b(g, carry):
        s = scale_v[g]
        rhs = res_v[:, lanes(g)]
        v = s * rhs + s * (rhs - product(win1, g))
        x_v[g] = v
        win2[nb + g] = v.astype(BF)
        return carry

    for q in range(QUARTERS):
        lax.fori_loop(q * step, (q + 1) * step, fine_b, 0, unroll=step)
        halo_start(win2, 1, q * step, step)

    coarse_in.wait()

    def convert(c, carry):
        for k in range(2):
            at = pl.multiple_of((2 * c + k) * cdev, cdev)
            cb_v[k, c] = coarse_v[:, pl.ds(at, cdev)].astype(BF).T
        return carry

    lax.fori_loop(0, nch, convert, 0, unroll=2)
    halo_wait(win2, 1)

    def residual(g, carry):
        fr_v[g] = res_v[:, lanes(g)] - product(win2, g)
        return carry

    lax.fori_loop(0, nb, residual, 0, unroll=min(32, nb))

    def restrict(c, acc):
        parts = []
        for k in range(4):
            g = 4 * c + k
            high = jnp.broadcast_to(lax.shift_right_logical(owner_row(g), 7), (cols, L))
            v = fr_v[g]
            parts.append(
                jnp.concatenate(
                    [jnp.where(high == h, v, 0.0).astype(BF) for h in range(nm)], axis=0
                )
            )
        return acc + dot(jnp.concatenate(parts, axis=1), oht[:, lanes(4 * c, 4)], NT)

    mid_rhs = lax.fori_loop(
        0, nb // 4, restrict, jnp.zeros((nm * cols, L), F32), unroll=nb // 4
    ).reshape(nm, cols, L)

    mrhs[2 : nm + 2] = mid_rhs
    rhs_edges = edge_copies(mrhs, 2, 2, msend, mrecv)
    for copy, when in rhs_edges:
        send(copy, when)

    def inside(v, left_side):
        keep = r > 0 if left_side else r < rows - 1
        return jnp.where(keep, v, jnp.zeros_like(v))

    def mid_product(mwin, g, before):
        v3 = jnp.concatenate([mwin[before + k] for k in range(3)], axis=1)
        t3 = jnp.concatenate([mid_v[g, k] for k in range(3)], axis=0)
        return dot(v3, t3, NN)

    mb = [None] * (nm + 2)

    def mid_b(g):
        s = ms_v[g + 1]
        rhs = mrhs[g + 1]
        mb[g] = s * rhs + s * (rhs - mid_product(mwin1, g, g))

    for g in range(2, nm + 2):
        mwin1[g] = (ms_v[g] * mrhs[g]).astype(BF)
    for g in range(2, nm):
        mid_b(g)
    for copy, when in (*edges, *rhs_edges):
        received(copy, when)
    for g in (0, 1, nm + 2, nm + 3):
        mwin1[g] = inside(ms_v[g] * mrhs[g], g < 2).astype(BF)
    for g in (0, 1, nm, nm + 1):
        mid_b(g)
    for g in range(nm + 2):
        v = mb[g]
        if g in (0, nm + 1):
            v = inside(v, g == 0)
        mwin2[g] = v.astype(BF)
    mid_res = [mrhs[g + 1] - mid_product(mwin2, g, g - 1) for g in range(1, nm + 1)]

    flat = jnp.concatenate(mid_res, axis=1)
    hot2 = jnp.concatenate([oh2t[1 + g] for g in range(nm)], axis=1)
    both = dot(jnp.concatenate(split(flat), axis=0), hot2, NT)
    partial = both[:cols] + both[cols:]
    even, odd = partial[:, :cdev], partial[:, cdev:]
    pair1[0] = jnp.where(core == 0, odd, even)
    swap1 = remote(pair1.at[0], pair1.at[1], psend.at[0], precv.at[0], {"rows": partner})
    send(swap1)
    swap1.wait_recv()
    coarse_rhs = jnp.where(core == 0, even, odd) + pair1[1]

    ag[core, chip] = coarse_rhs.astype(BF)

    for d in steps:
        to = 2 * chip_at(*d) + core
        remote(ag.at[core, chip], ag.at[core, chip], ags.at[0], agr.at[0], {"rows": to}).start()

    ag_all = remote(
        ag.at[core, pl.ds(0, nch - 1)], ag.at[core, pl.ds(0, nch - 1)],
        ags.at[0], agr.at[0], {"rows": partner},
    )
    pending.append((ag_all, None))
    ag_all.wait_recv()
    half = remote(ag.at[core], ag.at[core], ags.at[1], agr.at[1], {"rows": partner})
    send(half)

    def coarse_half(k, acc):
        def chunk(c, acc):
            v = jnp.concatenate([ag[k, 4 * c + i] for i in range(4)], axis=1)
            t = jnp.concatenate([cb_v[k, 4 * c + i] for i in range(4)], axis=0)
            return acc + dot(v, t, NN)

        return lax.fori_loop(0, nch // 4, chunk, acc, unroll=nch // 4)

    fix = coarse_half(core, jnp.zeros((cols, cdev), F32))
    half.wait_recv()
    fix = coarse_half(1 - core, fix)

    fx[0] = fix
    fix_out = [
        remote(fx.at[0], fx.at[1 + k], fs.at[k], fr.at[k], {"rows": to})
        for k, to in enumerate((partner, outer, outer2))
    ]
    last_but = jnp.logical_and(r != 1, r != rows - 2)
    for copy, when in zip(fix_out[::-1], (last_but, bordered, None)):
        send(copy, when)

    def halves(a, b):
        return jnp.concatenate([jnp.where(core == 0, a, b), jnp.where(core == 0, b, a)], axis=1)

    def lifted(values, hots):
        both = dot(jnp.concatenate(split(values), axis=0), hots, NN)
        return both[:cols] + both[cols:]

    def mid_c(g, lift):
        mb[g] = mb[g] + lift
        v = mb[g]
        if g in (0, nm + 1):
            v = inside(v, g == 0)
        mwin3[g] = v.astype(BF)

    def mid_d(g):
        mb[g] = mb[g] + ms_v[g + 1] * (mrhs[g + 1] - mid_product(mwin3, g, g - 1))

    fix_out[0].wait_recv()
    pair = halves(fix, fx[1])
    lift = lifted(pair, hot2)
    for g in range(1, nm + 1):
        mid_c(g, lift[:, (g - 1) * L : g * L])
    for g in range(2, nm):
        mid_d(g)
    for copy in fix_out[1:]:
        received(copy, bordered)
    pair2 = halves(fx[3], fx[2])
    mid_c(0, lifted(jnp.where(core == 0, pair2, pair), oh2t[0]))
    mid_c(nm + 1, lifted(jnp.where(core == 0, pair, pair2), oh2t[nm + 1]))
    mid_d(1)
    mid_d(nm)

    md = jnp.concatenate(mb[1 : nm + 1], axis=0)
    cw[...] = jnp.concatenate(split(md), axis=1)

    wide = min(8, step)

    def prolong(c, carry):
        hots = oht[:, lanes(wide * c, wide)]
        up = dot(cw[...], jnp.concatenate([hots, hots], axis=0), NN)
        for k in range(wide):
            g = wide * c + k
            high = jnp.broadcast_to(lax.shift_right_logical(owner_row(g), 7), (cols, L))
            v = x_v[g]
            for h in range(nm):
                v = v + jnp.where(
                    high == h, up[h * cols : (h + 1) * cols, k * L : (k + 1) * L], 0.0
                )
            x_v[g] = v
            win3[nb + g] = v.astype(BF)
        return carry

    each = step // wide
    for q in range(QUARTERS):
        lax.fori_loop(q * each, (q + 1) * each, prolong, 0, unroll=each)
        halo_start(win3, 2, q * step, step)
    halo_wait(win3, 2)

    def finish(g, carry):
        v = x_v[g] + scale_v[g] * (res_v[:, lanes(g)] - product(win3, g))
        dir_v[:, lanes(g)] = v
        dirb[:, lanes(g)] = v.astype(BF)
        return carry

    def dir_out(q):
        at = pl.ds(q * (nb // 2) * L, (nb // 2) * L)
        return pltpu.make_async_copy(dir_v.at[:, at], dir_ref.at[:, at], dsem.at[q])

    for q in range(2):
        lax.fori_loop(q * (nb // 2), (q + 1) * (nb // 2), finish, 0, unroll=nb // 2)
        dir_out(q).start()

    basis_all.wait_recv()

    def gram(c, acc):
        t = basis_v[:, :, lanes(4 * c, 4)].reshape(nx * cols, 4 * L)
        return acc + dot(dirb[:, lanes(4 * c, 4)], t, NT)

    total = lax.fori_loop(
        0, nb // 4, gram, jnp.zeros((cols, nx * cols), F32), unroll=nb // 4
    )
    rows8 = cols // 2
    ga[core] = jnp.concatenate([total[:rows8], total[rows8:]], axis=1)
    swap3 = remote(ga.at[core], ga.at[core], gs.at[0], gr.at[0], {"rows": partner})
    send(swap3)
    swap3.wait_recv()
    gd[chip] = ga[0] + ga[1]

    for d in steps:
        to = 2 * chip_at(*d) + core
        remote(gd.at[chip], gd.at[chip], gs.at[1], gr.at[1], {"rows": to}).start()

    gd_all = remote(
        gd.at[pl.ds(0, nch - 1)], gd.at[pl.ds(0, nch - 1)], gs.at[1], gr.at[1], {"rows": partner}
    )
    pending.append((gd_all, None))
    gd_all.wait_recv()
    parts = [gd[k] for k in range(nch)]
    while len(parts) > 1:
        parts = [a + b for a, b in zip(parts[::2], parts[1::2])]
    acc = parts[0]
    wide = nx * cols
    gram_v[...] = jnp.concatenate([acc[:, :wide], acc[:, wide:]], axis=0)
    gram_out = local(gram_v, gram_ref, 0)
    gram_out.start()
    dir_out(0).wait()
    dir_out(1).wait()
    gram_out.wait()
    pending_done()


def place(a_ref, b_ref, a_out, b_out):
    a_out[...] = a_ref[...]
    b_out[...] = b_ref[...]


def on_device(ny, nz, nx, residual, basis, fine_tiles, fine_index, mid_tiles, fine_owner, mid_owner, coarse):
    nb = fine_tiles.shape[0]
    nm = mid_tiles.shape[0]
    cols = residual.shape[1]
    cdev = coarse.shape[0]
    n = nb * L
    nch = ny * nz
    vm, dma = pltpu.VMEM, pltpu.SemaphoreType.DMA
    scratch = [
        vm((cols, n), F32), vm((nb, 4, L, L), BF), vm((nm + 2, 3, L, L), BF),
        vm((nb, L), jnp.int32), vm((nm, L), jnp.int32),
        vm(coarse.shape, F32), vm((2, nch, cdev, cdev), BF), vm((nx, cols, n), BF),
        vm((nb, cols, L), F32), vm((nb, cols, L), F32), vm((nb, cols, L), F32),
        vm((3 * nb, cols, L), BF), vm((3 * nb, cols, L), BF), vm((3 * nb, cols, L), BF),
        vm((L, n), BF), vm((nm + 2, 2 * cdev, L), BF), vm((nm + 4, cols, L), F32),
        vm((nm + 4, cols, L), F32),
        vm((nm + 4, cols, L), BF), vm((nm + 2, cols, L), BF), vm((nm + 2, cols, L), BF),
        vm((2, cols, cdev), F32), vm((4, cols, cdev), F32), vm((2, nch, cols, cdev), BF),
        vm((nm * cols, 2 * L), BF), vm((cols, n), BF),
        vm((2, cols // 2, 2 * nx * cols), F32), vm((nch, cols // 2, 2 * nx * cols), F32),
        vm((cols, n), F32), vm((cols, nx * cols), F32),
        dma((8,)), dma((QUARTERS,)), dma((3, 2)), dma((3, 2)), dma((3, 2)), dma((3, 2)),
        dma((2,)), dma((2,)), dma((1,)), dma((1,)), dma((3,)), dma((3,)),
        dma((2,)), dma((2,)), dma, dma, dma((2,)), dma((2,)),
    ]
    hbm = pl.BlockSpec(memory_space=pl.ANY)
    directions, gram = pl.pallas_call(
        functools.partial(kernel, ny, nz, nx),
        out_shape=(
            jax.ShapeDtypeStruct((cols, n), F32),
            jax.ShapeDtypeStruct((cols, nx * cols), F32),
        ),
        in_specs=[hbm, hbm, hbm, pl.BlockSpec(memory_space=pltpu.SMEM), hbm, hbm, hbm, hbm],
        out_specs=(hbm, hbm),
        scratch_shapes=scratch,
        name="vcycle",
        compiler_params=pltpu.CompilerParams(
            collective_id=0, has_side_effects=True, vmem_limit_bytes=56 * 2**20
        ),
    )(
        residual.T, basis.T, fine_tiles, fine_index.T, mid_tiles,
        fine_owner.reshape(nb, L), mid_owner.reshape(nm, L), coarse,
    )
    directions, gram = pl.pallas_call(
        place,
        out_shape=(
            jax.ShapeDtypeStruct((cols, n), F32),
            jax.ShapeDtypeStruct((cols, nx * cols), F32),
        ),
        grid=(2,),
        in_specs=[pl.BlockSpec((cols, n // 2), lambda i: (0, i)), pl.BlockSpec((cols, nx * cols), lambda i: (0, 0))],
        out_specs=(pl.BlockSpec((cols, n // 2), lambda i: (0, i)), pl.BlockSpec((cols, nx * cols), lambda i: (0, 0))),
        name="place",
    )(directions, gram)
    return directions.T, gram.T


def solution(mesh, ny=4, nz=8):
    in_specs = (
        P("rows", "cols"),
        P("rows", "cols"),
        P("rows", None, None, None),
        P("rows", None),
        P("rows", None, None, None),
        P("rows"),
        P("rows"),
        P("rows", None),
    )
    out_specs = (P("rows", "cols"), P(None, "cols"))
    return jax.shard_map(
        functools.partial(on_device, ny, nz, mesh.shape["cols"]),
        mesh=mesh, in_specs=in_specs, out_specs=out_specs, check_vma=False,
    )
```

```python
import functools

import jax
import jax.numpy as jnp
from jax import lax
from jax.experimental import pallas as pl
from jax.experimental.pallas import tpu as pltpu
from jax.sharding import PartitionSpec as P

W = 0.6666666666666666
NT = (((1,), (1,)), ((), ()))
NN = (((1,), (0,)), ((), ()))
F32 = jnp.float32
BF = jnp.bfloat16
L = 128
QUARTERS = 4


def dot(a, b, dims):
    return lax.dot_general(a, b, dims, preferred_element_type=F32)


def split(x):
    high = x.astype(BF)
    return high, (x - high.astype(F32)).astype(BF)


def kernel(
    ny, nz, nx,
    res_hbm, basis_hbm, tiles_hbm, idx_ref, mid_hbm, own_hbm, mown_hbm, coarse_hbm,
    dir_ref, gram_ref,
    res_v, tiles_v, mid_v, own_v, mown_v, coarse_v, cb_v, basis_v, scale_v, x_v, fr_v,
    win1, win2, win3, oht, oh2t, ms_v, mrhs, mwin1, mwin2, mwin3, pair1, fx, ag, cw, dirb,
    ga, gd, dir_v, gram_v,
    lsem, dsem, hs, hr, es, er, msend, mrecv, psend, precv, fs, fr, ags, agr, bs, br, gs, gr,
):
    nb = tiles_v.shape[0]
    nm = mid_v.shape[0] - 2
    nch = ny * nz
    rows = 2 * nch
    cdev = coarse_v.shape[0]
    cols = res_v.shape[0]
    r = lax.axis_index("rows")
    x = lax.axis_index("cols")
    core = lax.rem(r, 2)
    chip = r // 2
    partner = 2 * chip + 1 - core
    outer = lax.rem(r + 2 * core - 1 + rows, rows)
    outer2 = 2 * lax.rem(chip + 1 - 2 * core + nch, nch) + core
    step = nb // QUARTERS

    def remote(src, dst, ssem, rsem, where):
        return pltpu.make_async_remote_copy(
            src_ref=src, dst_ref=dst, send_sem=ssem, recv_sem=rsem,
            device_id=where, device_id_type=pl.DeviceIdType.MESH,
        )

    def local(src, dst, k):
        return pltpu.make_async_copy(src, dst, lsem.at[k])

    def lanes(g, n=1):
        return pl.ds(pl.multiple_of(g * L, L), n * L)

    pending = []
    bordered = jnp.logical_and(r > 0, r < rows - 1)

    def guarded(when, act):
        if when is None:
            act()
        else:
            pl.when(when)(act)

    def send(copy, when=None):
        guarded(when, copy.start)
        pending.append((copy, when))

    def received(copy, when=None):
        guarded(when, copy.wait_recv)

    def pending_done():
        for copy, when in pending:
            guarded(when, copy.wait_send)

    def diag_in(q):
        at = pl.ds(q * step, step)
        return pltpu.make_async_copy(tiles_hbm.at[at, 0], tiles_v.at[at, 0], dsem.at[q])

    res_in = local(res_hbm, res_v, 1)
    off_in = local(tiles_hbm.at[:, 1:4], tiles_v.at[:, 1:4], 2)
    own_in = local(own_hbm, own_v, 3)
    mown_in = local(mown_hbm, mown_v, 4)
    mid_in = local(mid_hbm, mid_v.at[pl.ds(1, nm)], 5)
    coarse_in = local(coarse_hbm, coarse_v, 6)
    basis_in = local(basis_hbm, basis_v.at[x], 7)
    barrier = pltpu.get_barrier_semaphore()

    def greet(where):
        pl.semaphore_signal(
            barrier, inc=1, device_id=where, device_id_type=pl.DeviceIdType.MESH
        )

    greet({"rows": partner})
    greet({"rows": outer})

    @pl.loop(1, nch)
    def _(d):
        greet({"rows": 2 * lax.rem(chip + d, nch) + core})

    @pl.loop(1, nx)
    def _(d):
        greet({"cols": lax.rem(x + d, nx)})

    res_in.start()
    for q in range(QUARTERS):
        diag_in(q).start()
    for copy in (mid_in, own_in, mown_in, off_in, coarse_in, basis_in):
        copy.start()

    eye = lax.broadcasted_iota(jnp.int32, (L, L), 0) == lax.broadcasted_iota(
        jnp.int32, (L, L), 1
    )

    def weight(tile):
        d = jnp.sum(jnp.where(eye, tile.astype(F32), 0.0), axis=0, keepdims=True)
        return jnp.broadcast_to(W * (1.0 / d), (cols, L))

    far_part = 2 * nb * (1 - core)
    near_part = 2 * nb * core

    def halo(win, k, lo, n):
        own = win.at[pl.ds(nb + lo, n)]
        return (
            (remote(own, win.at[pl.ds(far_part + lo, n)], hs.at[k, 0], hr.at[k, 0], {"rows": outer}), bordered),
            (remote(own, win.at[pl.ds(near_part + lo, n)], hs.at[k, 1], hr.at[k, 1], {"rows": partner}), None),
        )

    def halo_start(win, k, lo, n):
        for copy, when in halo(win, k, lo, n):
            guarded(when, copy.start)
        if lo == 0:
            pending.extend(halo(win, k, 0, nb))

    def halo_wait(win, k):
        for copy, when in halo(win, k, 0, nb):
            received(copy, when)

    yc = chip // nz
    zc = lax.rem(chip, nz)
    steps = sorted(
        ((dy, dz) for dy in range(ny) for dz in range(nz) if dy or dz),
        key=lambda d: -min(d[0], ny - d[0]) - min(d[1], nz - d[1]),
    )

    def chip_at(dy, dz):
        return lax.rem(yc + dy, ny) * nz + lax.rem(zc + dz, nz)

    def first(g, carry):
        s = weight(tiles_v[g, 0])
        scale_v[g] = s
        win1[nb + g] = (s * res_v[:, lanes(g)]).astype(BF)
        return carry

    res_in.wait()
    for q in range(QUARTERS):
        diag_in(q).wait()
        lax.fori_loop(q * step, (q + 1) * step, first, 0, unroll=min(8, step))
        if q == 0:
            pl.semaphore_wait(barrier, nch - 1 + 2 + nx - 1)
        halo_start(win1, 0, q * step, step)

    basis_in.wait()

    def basis_copy(d):
        return remote(
            basis_v.at[x], basis_v.at[x], bs, br, {"cols": lax.rem(x + d, nx)}
        )

    @pl.loop(1, nx)
    def _(d):
        basis_copy(d).start()

    basis_all = remote(
        basis_v.at[pl.ds(0, nx - 1)], basis_v.at[pl.ds(0, nx - 1)], bs, br,
        {"rows": partner},
    )
    pending.append((basis_all, None))

    mid_in.wait()
    mown_in.wait()
    wide_iota = lax.broadcasted_iota(jnp.int32, (2 * cdev, L), 0)
    mid_base = (r - core) * cdev
    for g in range(nm):
        oh2t[1 + g] = jnp.where(
            wide_iota == mown_v[g : g + 1, :] - mid_base, 1.0, 0.0
        ).astype(BF)
        ms_v[2 + g] = weight(mid_v[1 + g, 1])
        for k in range(3):
            mid_v[1 + g, k] = mid_v[1 + g, k].T

    def edge_copies(buf, n, own, ssem, rsem):
        out_at = own + core * (nm - n)
        out_to = own + nm - core * (nm + n)
        in_at = own + (1 - core) * (nm - n)
        in_to = own - n + core * (nm + n)
        return (
            (remote(buf.at[pl.ds(out_at, n)], buf.at[pl.ds(out_to, n)], ssem.at[0], rsem.at[0], {"rows": outer}), bordered),
            (remote(buf.at[pl.ds(in_at, n)], buf.at[pl.ds(in_to, n)], ssem.at[1], rsem.at[1], {"rows": partner}), None),
        )

    edges = []
    for k, (buf, n, own) in enumerate(((mid_v, 1, 1), (oh2t, 1, 1), (ms_v, 2, 2))):
        edges.extend(edge_copies(buf, n, own, es.at[k], er.at[k]))
    for copy, when in edges:
        send(copy, when)

    low_iota = lax.broadcasted_iota(jnp.int32, (L, L), 0)
    fine_base = r * (nm * L)

    def owner_row(g):
        return own_v[pl.ds(g, 1), :] - fine_base

    def hot(g, carry):
        low = jnp.bitwise_and(owner_row(g), L - 1)
        oht[:, lanes(g)] = jnp.where(low_iota == low, 1.0, 0.0).astype(BF)
        return carry

    off_in.wait()

    def turn(g, carry):
        for s in range(4):
            tiles_v[g, s] = tiles_v[g, s].T
        return carry

    lax.fori_loop(0, nb, turn, 0, unroll=min(16, nb))
    halo_wait(win1, 0)
    base = (r - 1) * nb

    def product(win, g):
        picked = [win[nb + g]] + [
            win[jnp.clip(idx_ref[s, g] - base, 0, 3 * nb - 1)] for s in (1, 2, 3)
        ]
        tile = [tiles_v[g, s] for s in range(4)]
        return dot(jnp.concatenate(picked, axis=1), jnp.concatenate(tile, axis=0), NN)

    def fine_b(g, carry):
        s = scale_v[g]
        rhs = res_v[:, lanes(g)]
        v = s * rhs + s * (rhs - product(win1, g))
        x_v[g] = v
        win2[nb + g] = v.astype(BF)
        return carry

    ends = (0, step // 2, 3 * step // 2, 5 * step // 2, 7 * step // 2, nb)
    for lo, hi in zip(ends, ends[1:]):
        lax.fori_loop(lo, hi, fine_b, 0, unroll=hi - lo)
        halo_start(win2, 1, lo, hi - lo)

    coarse_in.wait()

    def convert(c, carry):
        for k in range(2):
            at = pl.multiple_of((2 * c + k) * cdev, cdev)
            cb_v[k, c] = coarse_v[:, pl.ds(at, cdev)].astype(BF).T
        return carry

    lax.fori_loop(0, nch, convert, 0, unroll=2)
    own_in.wait()
    lax.fori_loop(0, nb, hot, 0, unroll=4)
    halo_wait(win2, 1)

    def residual(g, carry):
        fr_v[g] = res_v[:, lanes(g)] - product(win2, g)
        return carry

    lax.fori_loop(0, nb, residual, 0, unroll=min(32, nb))

    def restrict(c, acc):
        parts = []
        for k in range(4):
            g = 4 * c + k
            high = jnp.broadcast_to(lax.shift_right_logical(owner_row(g), 7), (cols, L))
            v = fr_v[g]
            parts.append(
                jnp.concatenate(
                    [jnp.where(high == h, v, 0.0).astype(BF) for h in range(nm)], axis=0
                )
            )
        return acc + dot(jnp.concatenate(parts, axis=1), oht[:, lanes(4 * c, 4)], NT)

    mid_rhs = lax.fori_loop(
        0, nb // 4, restrict, jnp.zeros((nm * cols, L), F32), unroll=nb // 4
    ).reshape(nm, cols, L)

    mrhs[2 : nm + 2] = mid_rhs
    rhs_edges = edge_copies(mrhs, 2, 2, msend, mrecv)
    for copy, when in rhs_edges:
        send(copy, when)

    def inside(v, left_side):
        keep = r > 0 if left_side else r < rows - 1
        return jnp.where(keep, v, jnp.zeros_like(v))

    def mid_product(mwin, g, before):
        v3 = jnp.concatenate([mwin[before + k] for k in range(3)], axis=1)
        t3 = jnp.concatenate([mid_v[g, k] for k in range(3)], axis=0)
        return dot(v3, t3, NN)

    mb = [None] * (nm + 2)

    def mid_b(g):
        s = ms_v[g + 1]
        rhs = mrhs[g + 1]
        mb[g] = s * rhs + s * (rhs - mid_product(mwin1, g, g))

    for g in range(2, nm + 2):
        mwin1[g] = (ms_v[g] * mrhs[g]).astype(BF)
    for g in range(2, nm):
        mid_b(g)
    for copy, when in (*edges, *rhs_edges):
        received(copy, when)
    for g in (0, 1, nm + 2, nm + 3):
        mwin1[g] = inside(ms_v[g] * mrhs[g], g < 2).astype(BF)
    for g in (0, 1, nm, nm + 1):
        mid_b(g)
    for g in range(nm + 2):
        v = mb[g]
        if g in (0, nm + 1):
            v = inside(v, g == 0)
        mwin2[g] = v.astype(BF)
    mid_res = [mrhs[g + 1] - mid_product(mwin2, g, g - 1) for g in range(1, nm + 1)]

    flat = jnp.concatenate(mid_res, axis=1)
    hot2 = jnp.concatenate([oh2t[1 + g] for g in range(nm)], axis=1)
    both = dot(jnp.concatenate(split(flat), axis=0), hot2, NT)
    partial = both[:cols] + both[cols:]
    even, odd = partial[:, :cdev], partial[:, cdev:]
    pair1[0] = jnp.where(core == 0, odd, even)
    swap1 = remote(pair1.at[0], pair1.at[1], psend.at[0], precv.at[0], {"rows": partner})
    send(swap1)
    swap1.wait_recv()
    coarse_rhs = jnp.where(core == 0, even, odd) + pair1[1]

    ag[core, chip] = coarse_rhs.astype(BF)

    for d in steps:
        to = 2 * chip_at(*d) + core
        remote(ag.at[core, chip], ag.at[core, chip], ags.at[0], agr.at[0], {"rows": to}).start()

    ag_all = remote(
        ag.at[core, pl.ds(0, nch - 1)], ag.at[core, pl.ds(0, nch - 1)],
        ags.at[0], agr.at[0], {"rows": partner},
    )
    pending.append((ag_all, None))
    ag_all.wait_recv()
    half = remote(ag.at[core], ag.at[core], ags.at[1], agr.at[1], {"rows": partner})
    send(half)

    def coarse_half(k, acc):
        def chunk(c, acc):
            v = jnp.concatenate([ag[k, 4 * c + i] for i in range(4)], axis=1)
            t = jnp.concatenate([cb_v[k, 4 * c + i] for i in range(4)], axis=0)
            return acc + dot(v, t, NN)

        return lax.fori_loop(0, nch // 4, chunk, acc, unroll=nch // 4)

    fix = coarse_half(core, jnp.zeros((cols, cdev), F32))
    half.wait_recv()
    fix = coarse_half(1 - core, fix)

    fx[0] = fix
    fix_out = [
        remote(fx.at[0], fx.at[1 + k], fs.at[k], fr.at[k], {"rows": to})
        for k, to in enumerate((partner, outer, outer2))
    ]
    last_but = jnp.logical_and(r != 1, r != rows - 2)
    for copy, when in zip(fix_out[::-1], (last_but, bordered, None)):
        send(copy, when)

    def halves(a, b):
        return jnp.concatenate([jnp.where(core == 0, a, b), jnp.where(core == 0, b, a)], axis=1)

    def lifted(values, hots):
        both = dot(jnp.concatenate(split(values), axis=0), hots, NN)
        return both[:cols] + both[cols:]

    def mid_c(g, lift):
        mb[g] = mb[g] + lift
        v = mb[g]
        if g in (0, nm + 1):
            v = inside(v, g == 0)
        mwin3[g] = v.astype(BF)

    def mid_d(g):
        mb[g] = mb[g] + ms_v[g + 1] * (mrhs[g + 1] - mid_product(mwin3, g, g - 1))

    fix_out[0].wait_recv()
    pair = halves(fix, fx[1])
    lift = lifted(pair, hot2)
    for g in range(1, nm + 1):
        mid_c(g, lift[:, (g - 1) * L : g * L])
    for g in range(2, nm):
        mid_d(g)
    for copy in fix_out[1:]:
        received(copy, bordered)
    pair2 = halves(fx[3], fx[2])
    mid_c(0, lifted(jnp.where(core == 0, pair2, pair), oh2t[0]))
    mid_c(nm + 1, lifted(jnp.where(core == 0, pair, pair2), oh2t[nm + 1]))
    mid_d(1)
    mid_d(nm)

    md = jnp.concatenate(mb[1 : nm + 1], axis=0)
    cw[...] = jnp.concatenate(split(md), axis=1)

    wide = min(8, step)

    def prolong(c, carry):
        hots = oht[:, lanes(wide * c, wide)]
        up = dot(cw[...], jnp.concatenate([hots, hots], axis=0), NN)
        for k in range(wide):
            g = wide * c + k
            high = jnp.broadcast_to(lax.shift_right_logical(owner_row(g), 7), (cols, L))
            v = x_v[g]
            for h in range(nm):
                v = v + jnp.where(
                    high == h, up[h * cols : (h + 1) * cols, k * L : (k + 1) * L], 0.0
                )
            x_v[g] = v
            win3[nb + g] = v.astype(BF)
        return carry

    each = step // wide
    for q in range(QUARTERS):
        lax.fori_loop(q * each, (q + 1) * each, prolong, 0, unroll=each)
        halo_start(win3, 2, q * step, step)
    halo_wait(win3, 2)

    def finish(g, carry):
        v = x_v[g] + scale_v[g] * (res_v[:, lanes(g)] - product(win3, g))
        dir_v[:, lanes(g)] = v
        dirb[:, lanes(g)] = v.astype(BF)
        return carry

    def dir_out(q):
        at = pl.ds(q * (nb // 2) * L, (nb // 2) * L)
        return pltpu.make_async_copy(dir_v.at[:, at], dir_ref.at[:, at], dsem.at[q])

    for q in range(2):
        lax.fori_loop(q * (nb // 2), (q + 1) * (nb // 2), finish, 0, unroll=nb // 2)
        dir_out(q).start()

    basis_all.wait_recv()

    def gram(c, acc):
        t = basis_v[:, :, lanes(4 * c, 4)].reshape(nx * cols, 4 * L)
        return acc + dot(dirb[:, lanes(4 * c, 4)], t, NT)

    total = lax.fori_loop(
        0, nb // 4, gram, jnp.zeros((cols, nx * cols), F32), unroll=nb // 4
    )
    rows8 = cols // 2
    ga[core] = jnp.concatenate([total[:rows8], total[rows8:]], axis=1)
    swap3 = remote(ga.at[core], ga.at[core], gs.at[0], gr.at[0], {"rows": partner})
    send(swap3)
    swap3.wait_recv()
    gd[chip] = ga[0] + ga[1]

    for d in steps:
        to = 2 * chip_at(*d) + core
        remote(gd.at[chip], gd.at[chip], gs.at[1], gr.at[1], {"rows": to}).start()

    gd_all = remote(
        gd.at[pl.ds(0, nch - 1)], gd.at[pl.ds(0, nch - 1)], gs.at[1], gr.at[1], {"rows": partner}
    )
    pending.append((gd_all, None))
    gd_all.wait_recv()
    parts = [gd[k] for k in range(nch)]
    while len(parts) > 1:
        parts = [a + b for a, b in zip(parts[::2], parts[1::2])]
    acc = parts[0]
    wide = nx * cols
    gram_v[...] = jnp.concatenate([acc[:, :wide], acc[:, wide:]], axis=0)
    gram_out = local(gram_v, gram_ref, 0)
    gram_out.start()
    dir_out(0).wait()
    dir_out(1).wait()
    gram_out.wait()
    pending_done()


def place(a_ref, b_ref, a_out, b_out):
    a_out[...] = a_ref[...]
    b_out[...] = b_ref[...]


def on_device(ny, nz, nx, residual, basis, fine_tiles, fine_index, mid_tiles, fine_owner, mid_owner, coarse):
    nb = fine_tiles.shape[0]
    nm = mid_tiles.shape[0]
    cols = residual.shape[1]
    cdev = coarse.shape[0]
    n = nb * L
    nch = ny * nz
    vm, dma = pltpu.VMEM, pltpu.SemaphoreType.DMA
    scratch = [
        vm((cols, n), F32), vm((nb, 4, L, L), BF), vm((nm + 2, 3, L, L), BF),
        vm((nb, L), jnp.int32), vm((nm, L), jnp.int32),
        vm(coarse.shape, F32), vm((2, nch, cdev, cdev), BF), vm((nx, cols, n), BF),
        vm((nb, cols, L), F32), vm((nb, cols, L), F32), vm((nb, cols, L), F32),
        vm((3 * nb, cols, L), BF), vm((3 * nb, cols, L), BF), vm((3 * nb, cols, L), BF),
        vm((L, n), BF), vm((nm + 2, 2 * cdev, L), BF), vm((nm + 4, cols, L), F32),
        vm((nm + 4, cols, L), F32),
        vm((nm + 4, cols, L), BF), vm((nm + 2, cols, L), BF), vm((nm + 2, cols, L), BF),
        vm((2, cols, cdev), F32), vm((4, cols, cdev), F32), vm((2, nch, cols, cdev), BF),
        vm((nm * cols, 2 * L), BF), vm((cols, n), BF),
        vm((2, cols // 2, 2 * nx * cols), F32), vm((nch, cols // 2, 2 * nx * cols), F32),
        vm((cols, n), F32), vm((cols, nx * cols), F32),
        dma((8,)), dma((QUARTERS,)), dma((3, 2)), dma((3, 2)), dma((3, 2)), dma((3, 2)),
        dma((2,)), dma((2,)), dma((1,)), dma((1,)), dma((3,)), dma((3,)),
        dma((2,)), dma((2,)), dma, dma, dma((2,)), dma((2,)),
    ]
    hbm = pl.BlockSpec(memory_space=pl.ANY)
    directions, gram = pl.pallas_call(
        functools.partial(kernel, ny, nz, nx),
        out_shape=(
            jax.ShapeDtypeStruct((cols, n), F32),
            jax.ShapeDtypeStruct((cols, nx * cols), F32),
        ),
        in_specs=[hbm, hbm, hbm, pl.BlockSpec(memory_space=pltpu.SMEM), hbm, hbm, hbm, hbm],
        out_specs=(hbm, hbm),
        scratch_shapes=scratch,
        name="vcycle",
        compiler_params=pltpu.CompilerParams(
            collective_id=0, has_side_effects=True, vmem_limit_bytes=56 * 2**20
        ),
    )(
        residual.T, basis.T, fine_tiles, fine_index.T, mid_tiles,
        fine_owner.reshape(nb, L), mid_owner.reshape(nm, L), coarse,
    )
    directions, gram = pl.pallas_call(
        place,
        out_shape=(
            jax.ShapeDtypeStruct((cols, n), F32),
            jax.ShapeDtypeStruct((cols, nx * cols), F32),
        ),
        grid=(2,),
        in_specs=[pl.BlockSpec((cols, n // 2), lambda i: (0, i)), pl.BlockSpec((cols, nx * cols), lambda i: (0, 0))],
        out_specs=(pl.BlockSpec((cols, n // 2), lambda i: (0, i)), pl.BlockSpec((cols, nx * cols), lambda i: (0, 0))),
        name="place",
    )(directions, gram)
    return directions.T, gram.T


def solution(mesh, ny=4, nz=8):
    in_specs = (
        P("rows", "cols"),
        P("rows", "cols"),
        P("rows", None, None, None),
        P("rows", None),
        P("rows", None, None, None),
        P("rows"),
        P("rows"),
        P("rows", None),
    )
    out_specs = (P("rows", "cols"), P(None, "cols"))
    return jax.shard_map(
        functools.partial(on_device, ny, nz, mesh.shape["cols"]),
        mesh=mesh, in_specs=in_specs, out_specs=out_specs, check_vma=False,
    )
```
